32 devices in a mesh: comp: 2 (over core), tile: 16 (over z, y, x).
Axes of the slice: x: 2, y: 2, z: 4, core: 2. Of those that a mesh axis runs over, the one named last changes fastest.
Arguments:
- tracers: float32 [2, 16, 4, 512, 128], P('comp', None, None, 'tile'), may hold values from -6 to 6
- diffusion: float32 [2, 16, 4, 512, 128], P('comp', None, None, 'tile'), may hold values from 0.1 to 10
- coupling: float32 [2, 4, 512, 128], P('comp', None, 'tile'), may hold values from 0.2 to 5
- source: float32 [2, 4, 512, 128], P('comp', None, 'tile'), may hold values from -6 to 6
- sea_mask: int32 [2, 512, 128], P('comp', 'tile'), may hold values 0 or 1
- mixing: float32 [2, 4], P('comp'), may hold values from 0.05 to 0.2
- cell_counts: int32 [2, 16, 16], P('comp', 'tile'), may hold values from 0 to 1024, as said below
- cell_columns: int32 [2, 16, 16, 1024], P('comp', 'tile'), may hold values from 0 to 4095
- cell_areas: float32 [2, 16, 16, 1024], P('comp', 'tile'), may hold values from 0.05 to 1
Outputs:
- new_tracers: float32 [2, 16, 4, 512, 128], P('comp', None, None, 'tile')
- surface_flux: float32 [2, 4, 512, 128], P('comp', None, 'tile')
The draws below stay inside these ranges and needn't reach their ends.
Inputs may be any that keep to these rules, and one draw needn't show every extreme that they name: cell_counts[1] is the transpose of cell_counts[0]. In every draw some atmosphere block shares 1024 cells with every ocean block, and some ocean block shares 1024 cells with every atmosphere block. `cell_columns`: slots at or beyond the pair's count in cell_counts are not used.
All inputs are finite; a program needn't handle non-finite values. No bound on the sum of `sea_mask` on one device may be relied on, other than what follows from the above.
Results may differ from the reference program's by a relative error of at most 0.00005.
Values sent between devices are 32-bit elements; how exact they have to be, the bound alone decides.
A program may use at most 64 MiB of HBM per device.

```python
import math
import jax
import jax.numpy as jnp
from jax import lax

NF = 4
LEV = 16
RY = 32
RX = 128
CAP = 1024
TILES = 16
NY = 512


def counts_table(key):
    first, second, third, fourth = jax.random.split(jax.random.fold_in(key, 7), 4)
    base = jax.random.randint(first, (TILES, TILES), 0, CAP + 1)
    weight = jax.random.randint(second, (TILES, 1), 1, 5)
    table = base * weight // 4
    busy_row = jax.random.randint(third, (), 0, TILES)
    busy_col = jax.random.randint(fourth, (), 0, TILES)
    places = jnp.arange(TILES)
    filled = (places[:, None] == busy_row) | (places[None, :] == busy_col)
    return jnp.where(filled, CAP, table).astype(jnp.int32)


def draw_cell_counts(key, part):
    table = counts_table(key)
    return jnp.stack([table, table.T])


def set_ends(values, stream_key, smallest, top_value):
    index_at = [jax.random.randint(jax.random.fold_in(stream_key, axis), (), 0, length) for axis, length in enumerate(values.shape)]
    widest = values.shape.index(max(values.shape))
    beside = index_at[:widest] + [(index_at[widest] + 1) % values.shape[widest]] + index_at[widest + 1:]
    return values.at[tuple(index_at)].set(smallest).at[tuple(beside)].set(top_value)


def shard_levels(stream_key, extent, cuts, least, largest):
    level, own = 1.0, jax.random.fold_in(stream_key, 6)
    for position, shards_of in cuts:
        draws = jnp.exp(jax.random.uniform(jax.random.fold_in(own, position), (shards_of,), jnp.float32, least / len(cuts), largest / len(cuts)))
        level = level * jnp.repeat(draws, extent[position] // shards_of).reshape([-1 if axis == position else 1 for axis in range(len(extent))])
    return level


def noise(own_key, shape, scale, most, cuts=(), kind=jnp.bfloat16):
    values = jax.random.normal(own_key, shape, jnp.float32) * scale
    if len(cuts) > 0:
        values = shard_levels(own_key, shape, cuts, -0.22, 0.18) * values
    return jnp.clip(values, min=-most, max=most).astype(kind)


def setup_inputs(seed: int = 0) -> dict:
    streams_of = jax.random.split(jax.random.key(seed), 10)
    tracers = noise(streams_of[0], (2, LEV, NF, NY, RX), 1.0, 6.0, ((0, 2), (3, 16)), jnp.float32)
    diffusion = jnp.clip(jnp.exp(math.log(10.0) - 4.6051702 * jax.random.uniform(streams_of[1], (2, LEV, NF, NY, RX), jnp.float32) ** shard_levels(streams_of[1], (2, LEV, NF, NY, RX), ((0, 2), (3, 16)), -0.2, 0.2)), 0.1, 10.0)
    coupling = jnp.clip(jnp.exp(math.log(5.0) - 3.218876 * jax.random.uniform(streams_of[2], (2, NF, NY, RX), jnp.float32) ** shard_levels(streams_of[2], (2, NF, NY, RX), ((0, 2), (2, 16)), -0.2, 0.2)), 0.2, 5.0)
    source = noise(streams_of[3], (2, NF, NY, RX), 1.0, 6.0, ((0, 2), (2, 16)), jnp.float32)
    sea_mask = set_ends((jax.random.randint(streams_of[4], (2, NY, RX), 0, 4) < 3).astype(jnp.int32), jax.random.fold_in(streams_of[4], 1), 0, 1)
    mixing = jnp.clip(jnp.exp(math.log(0.2) - 1.3862944 * jax.random.uniform(streams_of[5], (2, NF), jnp.float32) ** shard_levels(streams_of[5], (2, NF), ((0, 2),), -0.2, 0.2)), 0.05, 0.2)
    cell_counts = draw_cell_counts(jax.random.fold_in(streams_of[9], 71), 0)
    cell_columns = set_ends(jax.random.randint(streams_of[7], (2, TILES, TILES, CAP), 0, RY * RX), jax.random.fold_in(streams_of[7], 1), 0, (RY * RX) - 1).astype(jnp.int32)
    cell_areas = jnp.clip(jnp.exp(math.log(1.0) - 2.9957323 * jax.random.uniform(streams_of[8], (2, TILES, TILES, CAP), jnp.float32) ** shard_levels(streams_of[8], (2, TILES, TILES, CAP), ((0, 2), (1, 16)), -0.2, 0.2)), 0.05, 1.0)
    return dict(tracers=tracers, diffusion=diffusion, coupling=coupling, source=source, sea_mask=sea_mask, mixing=mixing, cell_counts=cell_counts, cell_columns=cell_columns, cell_areas=cell_areas)


def down_sweep(forcing, diffuse):
    diffuse_next = jnp.concatenate([diffuse[1:], jnp.zeros_like(diffuse[:1])], axis=0)

    def advance(carry, inputs):
        factor_prev, reduced_prev, pivot_prev = carry
        source_now, diffuse_now, diffuse_below = inputs
        pivot = 1.0 + diffuse_now + diffuse_below - diffuse_now * factor_prev
        factor = diffuse_below / pivot
        reduced = (source_now + diffuse_now * reduced_prev) / pivot
        return (factor, reduced, pivot), (factor, reduced)

    zeros_plane = jnp.zeros(forcing.shape[1:], jnp.float32)
    ones_plane = jnp.ones(forcing.shape[1:], jnp.float32)
    final, (factor, reduced) = lax.scan(advance, (zeros_plane, zeros_plane, ones_plane), (forcing, diffuse, diffuse_next))
    return factor, reduced, final[2]


def up_sweep(factor, reduced, lowest):
    def advance(below, inputs):
        factor_now, reduced_now = inputs
        value = reduced_now + factor_now * below
        return value, value

    _, upper = lax.scan(advance, lowest, (factor[:-1], reduced[:-1]), reverse=True)
    return jnp.concatenate([upper, lowest[None]], axis=0)


def laplace(field):
    padded = jnp.pad(field, ((0, 0), (0, 0), (0, 0), (1, 1), (0, 0)))
    across = padded[:, :, :, 2:] + padded[:, :, :, :-2]
    along = jnp.roll(field, 1, 4) + jnp.roll(field, -1, 4)
    return (across + along) - 4.0 * field


def reference(tracers, diffusion, coupling, source, sea_mask, mixing, cell_counts, cell_columns, cell_areas):
    tile_count = cell_columns.shape[1]
    capacity = cell_columns.shape[3]
    levels, field_count = tracers.shape[1], tracers.shape[2]
    block_rows = tracers.shape[3] // tile_count
    row_cells = tracers.shape[4]
    columns = block_rows * row_cells

    def to_blocks(array):
        array = array.reshape(2, levels, field_count, tile_count, columns)
        return jnp.moveaxis(array, 3, 1).reshape(2 * tile_count, levels, field_count, columns)

    def surface_blocks(array):
        array = array.reshape(2, field_count, tile_count, columns)
        return jnp.moveaxis(array, 2, 1)

    tracer_blocks = to_blocks(tracers)
    diffuse_blocks = to_blocks(diffusion)

    def first_pass(inputs):
        forcing, diffuse = inputs
        factor, reduced, pivot = down_sweep(forcing, diffuse)
        return reduced[-1], 1.0 / pivot

    bottom, admittance = lax.map(first_pass, (tracer_blocks, diffuse_blocks))
    bottom = bottom.reshape(2, tile_count, field_count, columns)
    admittance = admittance.reshape(2, tile_count, field_count, columns)
    mask_value = sea_mask.astype(jnp.float32).reshape(2, tile_count, 1, columns)
    coupling_value = surface_blocks(coupling)
    source_value = surface_blocks(source)
    conductance = mask_value * coupling_value / (1.0 + coupling_value * admittance)
    offered = mask_value * (source_value + conductance * bottom)

    side_index = jnp.arange(2)[:, None, None, None]
    tile_index = jnp.arange(tile_count)[None, :, None, None]
    cond_own = conductance[side_index, tile_index, :, cell_columns]
    offer_own = offered[side_index, tile_index, :, cell_columns]
    bottom_own = bottom[side_index, tile_index, :, cell_columns]

    def partner(array):
        return jnp.swapaxes(array[::-1], 1, 2)

    skin = (offer_own + partner(offer_own)) / (cond_own + partner(cond_own) + 1.0)
    slots = jnp.arange(capacity)
    valid = (slots[None, None, None, :] < cell_counts[..., None]).astype(jnp.float32)
    cell_flux = cond_own * (skin - bottom_own) * (valid * cell_areas)[..., None]
    flux = jnp.zeros((2, tile_count, field_count, columns), jnp.float32)
    flux = flux.at[side_index, tile_index, :, cell_columns].add(cell_flux)

    def second_pass(inputs):
        forcing, diffuse, flux_block = inputs
        factor, reduced, pivot = down_sweep(forcing, diffuse)
        return up_sweep(factor, reduced, reduced[-1] + (1.0 / pivot) * flux_block)

    solved = lax.map(second_pass, (tracer_blocks, diffuse_blocks, flux.reshape(2 * tile_count, field_count, columns)))
    solved = solved.reshape(2, tile_count, levels, field_count, columns)
    solved = jnp.moveaxis(solved, 1, 3).reshape(tracers.shape)
    new_tracers = solved + mixing[:, None, :, None, None] * laplace(tracers)
    surface_flux = jnp.moveaxis(flux, 1, 2).reshape(coupling.shape)
    return new_tracers, surface_flux
```

```python
import functools

import jax
import jax.numpy as jnp
from jax import lax
from jax.experimental import pallas as pl
from jax.experimental.pallas import tpu as pltpu
from jax.sharding import PartitionSpec as P

MESH = pl.DeviceIdType.MESH
CHUNKS = 4
WIDE = 256
BATCH = 4


def split_two(values):
    high = values.astype(jnp.bfloat16).astype(jnp.float32)
    return high, values - high


def as_bf16(integers):
    return integers.astype(jnp.float32).astype(jnp.bfloat16)


def hot_of(cells, lanes, groups):
    row = cells // lanes
    group = row % groups
    inside = (row // groups) * lanes + cells % lanes
    place = as_bf16(lax.broadcasted_iota(jnp.int32, (WIDE, cells.shape[1]), 0))
    one, zero = jnp.ones((), jnp.bfloat16), jnp.zeros((), jnp.bfloat16)
    return jnp.where(place == as_bf16(inside), one, zero), group


def kernel(
    tiles,
    mixing_ref, counts_ref, tracers_hbm, diffusion_hbm, coupling_hbm, source_hbm, mask_hbm, cells_hbm, areas_hbm,
    base_ref, slope_ref, flux_ref,
    tracers_ref, diffusion_ref, coupling_ref, source_ref, mask_ref, cells_ref, areas_ref, load_sem,
    factor_ref, planes_ref, table_ref, table16_ref, own_ref, partner_ref, skin_ref, answer_ref, total_ref,
    edge_ref, halo_ref,
    send_sem, recv_sem, edge_send, edge_recv,
):
    levels, fields, rows, lanes = tracers_ref.shape
    capacity = cells_ref.shape[1]
    halves = WIDE // lanes
    groups = rows * lanes // WIDE
    width = 2 * fields
    dense = capacity // 2
    comp = lax.axis_index("comp")
    tile = lax.axis_index("tile")
    other = 1 - comp
    after = lax.rem(tile + 1, tiles)
    before = lax.rem(tile + tiles - 1, tiles)

    side = tiles // 2
    place_in_side = tile % side
    near_base = (tile // side) * side
    far_base = side - near_base

    def near_block(j):
        return near_base + (place_in_side + j) % side

    def asked_block(i):
        return far_base + (place_in_side + 1 + comp + 2 * i) % side

    def owned_block(i):
        return far_base + (place_in_side + comp + 2 * i) % side

    chunk = levels // CHUNKS

    def level_load(source, target, part, slot):
        span = pl.ds(part * chunk, chunk)
        return pltpu.make_async_copy(source.at[span], target.at[span], load_sem.at[slot])

    tracer_loads = [level_load(tracers_hbm, tracers_ref, c, c) for c in range(CHUNKS)]
    diffusion_loads = [level_load(diffusion_hbm, diffusion_ref, c, CHUNKS + c) for c in range(CHUNKS)]
    pairs = (
        (coupling_hbm, coupling_ref), (source_hbm, source_ref), (mask_hbm, mask_ref),
        (cells_hbm, cells_ref), (areas_hbm, areas_ref),
    )
    rest_loads = [
        pltpu.make_async_copy(held, target, load_sem.at[2 * CHUNKS + i]) for i, (held, target) in enumerate(pairs)
    ]
    for c in range(CHUNKS):
        diffusion_loads[c].start()
        if c >= 1:
            tracer_loads[c - 1].start()
    tracer_loads[CHUNKS - 1].start()
    for load in rest_loads:
        load.start()

    barrier = pltpu.get_barrier_semaphore()

    def greet(step, carry):
        pl.semaphore_signal(barrier, inc=1, device_id=(other, step), device_id_type=MESH)
        return carry

    lax.fori_loop(0, tiles, greet, 0)
    pl.semaphore_signal(barrier, inc=1, device_id=(comp, after), device_id_type=MESH)
    pl.semaphore_signal(barrier, inc=1, device_id=(comp, before), device_id_type=MESH)

    def down(k, carry):
        factor, reduced = carry
        here = diffusion_ref[k]
        below = diffusion_ref[k + 1]
        field = tracers_ref[k]
        inverse = 1.0 / (1.0 + here + below - here * factor)
        factor = below * inverse
        reduced = (field + here * reduced) * inverse
        factor_ref[k] = factor
        base_ref[k] = reduced
        edge_ref[0, k] = field[:, rows - 1, :]
        edge_ref[1, k] = field[:, 0, :]
        return factor, reduced

    zeros = jnp.zeros((fields, rows, lanes), jnp.float32)
    factor, reduced = zeros, zeros
    diffusion_loads[0].wait()
    for c in range(CHUNKS):
        if c + 1 < CHUNKS:
            diffusion_loads[c + 1].wait()
        tracer_loads[c].wait()
        end = min((c + 1) * chunk, levels - 1)
        factor, reduced = lax.fori_loop(c * chunk, end, down, (factor, reduced))
    for load in rest_loads:
        load.wait()
    last = levels - 1
    here = diffusion_ref[last]
    field = tracers_ref[last]
    admittance = 1.0 / (1.0 + here - here * factor)
    bottom = (field + here * reduced) * admittance
    edge_ref[0, last] = field[:, rows - 1, :]
    edge_ref[1, last] = field[:, 0, :]
    base_ref[last] = bottom
    slope_ref[last] = admittance
    mask = mask_ref[...].astype(jnp.float32)[None]
    coupling = coupling_ref[...]
    conductance = mask * coupling / (1.0 + coupling * admittance)
    offered = mask * (source_ref[...] + conductance * bottom)
    for k in range(width):
        plane = offered[k] if k < fields else conductance[k - fields]
        for half in range(halves):
            table_ref[half, pl.ds(k, groups, stride=width), :] = plane[half * groups : (half + 1) * groups]
    table = jnp.concatenate([table_ref[half] for half in range(halves)], axis=1)
    high, low = split_two(table.reshape(groups, width, WIDE))
    table16_ref[...] = (
        jnp.concatenate([high, low], axis=1).reshape(groups * 2 * width, WIDE).astype(jnp.bfloat16)
    )

    edge_up = pltpu.make_async_remote_copy(
        src_ref=edge_ref.at[0], dst_ref=halo_ref.at[0], send_sem=edge_send.at[0], recv_sem=edge_recv.at[0],
        device_id=(comp, after), device_id_type=MESH,
    )
    edge_down = pltpu.make_async_remote_copy(
        src_ref=edge_ref.at[1], dst_ref=halo_ref.at[1], send_sem=edge_send.at[1], recv_sem=edge_recv.at[1],
        device_id=(comp, before), device_id_type=MESH,
    )
    has_before, has_after = tile > 0, tile < tiles - 1

    def block_copy(block, slot):
        return pltpu.make_async_remote_copy(
            src_ref=own_ref.at[block], dst_ref=partner_ref.at[slot],
            send_sem=send_sem.at[block], recv_sem=recv_sem.at[slot],
            device_id=(other, block), device_id_type=MESH,
        )

    def answer_copy(block, slot):
        return pltpu.make_async_remote_copy(
            src_ref=skin_ref.at[block], dst_ref=answer_ref.at[slot],
            send_sem=send_sem.at[block], recv_sem=recv_sem.at[slot],
            device_id=(other, block), device_id_type=MESH,
        )

    def cells_of(block):
        return hot_of(cells_ref[pl.ds(block, 1), :], lanes, groups)

    def pick(blocks):
        hots, group = zip(*[cells_of(block) for block in blocks])
        found = jnp.dot(table16_ref[...], jnp.concatenate(hots, axis=1), preferred_element_type=jnp.float32)
        size = 2 * width
        chosen = [
            found[g * size : g * size + width] + found[g * size + width : (g + 1) * size] for g in range(groups)
        ]
        group = jnp.broadcast_to(jnp.concatenate(group, axis=1), (width, len(blocks) * capacity))
        stride = 1
        while len(chosen) > 1:
            odd = (group // stride) % 2 == 1
            chosen = [jnp.where(odd, chosen[i + 1], chosen[i]) for i in range(0, len(chosen), 2)]
            stride *= 2
        for i, block in enumerate(blocks):
            own_ref[block] = chosen[0][:, i * capacity : (i + 1) * capacity]

    def each(count, batch, block_of, do):
        def step(s, carry):
            do([block_of(s * batch + i) for i in range(batch)])
            return carry

        if count == batch:
            step(0, 0)
        else:
            lax.fori_loop(0, count // batch, step, 0)

    def pick_and_send(blocks):
        pick(blocks)
        for block in blocks:
            block_copy(block, tile).start()

    far_batch = min(BATCH, side // 2)
    near_batch = min(BATCH, side)

    each(side // 2, far_batch, asked_block, pick)

    pl.semaphore_wait(barrier, tiles + 2)

    def send(step, carry):
        block_copy(asked_block(step), tile).start()
        return carry

    lax.fori_loop(0, side // 2, send, 0)

    @pl.when(has_after)
    def _():
        edge_up.start()

    @pl.when(has_before)
    def _():
        edge_down.start()

    each(side // 2, far_batch, owned_block, pick)
    each(side, near_batch, near_block, pick_and_send)

    upper = lax.broadcasted_iota(jnp.int32, (width, dense), 0) < fields

    def skin_of(block):
        both = own_ref[block] + partner_ref[block]
        turned = pltpu.roll(both, fields, 0)
        offers = jnp.where(upper, both[:, :dense], turned[:, dense:])
        conducts = jnp.where(upper, turned[:, :dense], both[:, dense:])
        return offers / (conducts + 1.0)

    def answer(step, carry):
        block = owned_block(step)
        block_copy(block, block).wait_recv()
        skin_ref[block] = skin_of(block)
        answer_copy(block, tile).start()
        return carry

    lax.fori_loop(0, side // 2, answer, 0)

    @pl.when(has_after)
    def _():
        edge_up.wait_send()
        edge_down.wait_recv()

    @pl.when(has_before)
    def _():
        edge_down.wait_send()
        edge_up.wait_recv()

    @pl.when(tile == 0)
    def _():
        halo_ref[0] = jnp.zeros((levels, fields, lanes), jnp.float32)

    @pl.when(tile == tiles - 1)
    def _():
        halo_ref[1] = jnp.zeros((levels, fields, lanes), jnp.float32)

    row = lax.broadcasted_iota(jnp.int32, (fields, rows, lanes), 1)
    first_row = row == 0
    last_row = row == rows - 1
    which = lax.broadcasted_iota(jnp.int32, (fields, rows, lanes), 0)
    mix = jnp.zeros((fields, rows, lanes), jnp.float32)
    for f in range(fields):
        mix = jnp.where(which == f, mixing_ref[f], mix)

    def spread(k):
        field = tracers_ref[k]
        north = jnp.where(first_row, halo_ref[0, k][:, None, :], pltpu.roll(field, 1, 1))
        south = jnp.where(last_row, halo_ref[1, k][:, None, :], pltpu.roll(field, rows - 1, 1))
        along = pltpu.roll(field, 1, 2) + pltpu.roll(field, lanes - 1, 2)
        return mix * (north + south + along - 4.0 * field)

    base_ref[last] = bottom + spread(last)

    def up(step, carry):
        base, slope = carry
        k = levels - 2 - step
        factor = factor_ref[k]
        base = base_ref[k] + factor * base
        slope = factor * slope
        slope_ref[k] = slope
        base_ref[k] = base + spread(k)
        return base, slope

    lax.fori_loop(0, levels - 1, up, (bottom, admittance))

    total_ref[...] = jnp.zeros_like(total_ref)
    slot_of = lax.broadcasted_iota(jnp.int32, (1, capacity), 1)
    group_of = as_bf16(lax.broadcasted_iota(jnp.int32, (groups, capacity), 0))

    def scatter(blocks, skins):
        hots, lefts = [], []
        for block, skin in zip(blocks, skins):
            hot, group = cells_of(block)
            here = group_of == as_bf16(group)
            area = jnp.where(slot_of < counts_ref[block], areas_ref[pl.ds(block, 1), :], 0.0)
            weight = skin * jnp.where(upper, area[:, :dense], area[:, dense:])
            pieces = []
            for part, area_part in zip(split_two(weight), split_two(area)):
                found = [
                    jnp.concatenate([part[f : f + 1], part[fields + f : fields + f + 1]], axis=1)
                    for f in range(fields)
                ]
                for value in found + [area_part]:
                    spread_value = jnp.broadcast_to(value, (groups, capacity)).astype(jnp.bfloat16)
                    pieces.append(jnp.where(here, spread_value, jnp.zeros((), jnp.bfloat16)))
            hots.append(hot)
            lefts.append(jnp.concatenate(pieces, axis=0))
        total_ref[...] += lax.dot_general(
            jnp.concatenate(hots, axis=1), jnp.concatenate(lefts, axis=1), (((1,), (1,)), ((), ())),
            preferred_element_type=jnp.float32,
        )

    def scatter_owned(blocks):
        scatter(blocks, [skin_ref[block] for block in blocks])

    def scatter_near(blocks):
        for block in blocks:
            block_copy(block, block).wait_recv()
        scatter(blocks, [skin_of(block) for block in blocks])

    def scatter_asked(blocks):
        for block in blocks:
            answer_copy(block, block).wait_recv()
        scatter(blocks, [answer_ref[block] for block in blocks])

    each(side // 2, far_batch, owned_block, scatter_owned)
    each(side, near_batch, near_block, scatter_near)
    each(side // 2, far_batch, asked_block, scatter_asked)

    sums = (fields + 1) * groups
    totals = total_ref[...].T
    totals = totals[:sums] + totals[sums:]
    for k in range(fields + 1):
        for half in range(halves):
            planes_ref[k, half * groups : (half + 1) * groups, :] = totals[
                k * groups : (k + 1) * groups, half * lanes : (half + 1) * lanes
            ]
    flux_ref[...] = conductance * (planes_ref[0:fields] - bottom * planes_ref[fields : fields + 1])

    def drain(step, carry):
        block_copy(asked_block(step), tile).wait_send()
        answer_copy(owned_block(step), tile).wait_send()
        return carry

    def drain_near(step, carry):
        block_copy(near_block(step), tile).wait_send()
        return carry

    lax.fori_loop(0, side // 2, drain, 0)
    lax.fori_loop(0, side, drain_near, 0)


def finish(base_ref, slope_ref, flux_ref, solved_hbm, surface_hbm, solved_ref, store_sem):
    chunk = base_ref.shape[0] // CHUNKS
    flux_store = pltpu.make_async_copy(flux_ref, surface_hbm, store_sem.at[CHUNKS])
    flux_store.start()
    flux = flux_ref[...]
    stores = []
    for c in range(CHUNKS):
        span = pl.ds(c * chunk, chunk)

        def combine(k, carry):
            solved_ref[k] = base_ref[k] + slope_ref[k] * flux
            return carry

        lax.fori_loop(c * chunk, (c + 1) * chunk, combine, 0, unroll=True)
        stores.append(pltpu.make_async_copy(solved_ref.at[span], solved_hbm.at[span], store_sem.at[c]))
        stores[-1].start()
    flux_store.wait()
    for store in stores:
        store.wait()


def on_device(
    tracers, diffusion, coupling, source, sea_mask, mixing, cell_counts, cell_columns, cell_areas
):
    levels, fields, rows, lanes = tracers.shape[1:]
    tiles, capacity = cell_columns.shape[2:]
    width = 2 * fields
    groups = rows * lanes // WIDE
    f32 = jnp.float32
    grid = jax.ShapeDtypeStruct((levels, fields, rows, lanes), f32)
    vmem = pl.BlockSpec(memory_space=pltpu.VMEM)
    smem = pl.BlockSpec(memory_space=pltpu.SMEM)
    held = [
        pltpu.with_memory_space_constraint(array, pltpu.HBM)
        for array in (
            tracers[0], diffusion[0], coupling[0], source[0], sea_mask[0], cell_columns[0, 0], cell_areas[0, 0]
        )
    ]
    base, slope, flux = pl.pallas_call(
        functools.partial(kernel, tiles),
        out_shape=(grid, grid, jax.ShapeDtypeStruct((fields, rows, lanes), f32)),
        in_specs=[smem, smem] + [pl.BlockSpec(memory_space=pltpu.HBM)] * 7,
        out_specs=(vmem, vmem, vmem),
        scratch_shapes=[
            pltpu.VMEM((levels, fields, rows, lanes), f32),
            pltpu.VMEM((levels, fields, rows, lanes), f32),
            pltpu.VMEM((fields, rows, lanes), f32),
            pltpu.VMEM((fields, rows, lanes), f32),
            pltpu.VMEM((rows, lanes), jnp.int32),
            pltpu.VMEM((tiles, capacity), jnp.int32),
            pltpu.VMEM((tiles, capacity), f32),
            pltpu.SemaphoreType.DMA((2 * CHUNKS + 5,)),
            pltpu.VMEM((levels, fields, rows, lanes), f32),
            pltpu.VMEM((fields + 1, rows, lanes), f32),
            pltpu.VMEM((WIDE // lanes, groups * width, lanes), f32),
            pltpu.VMEM((groups * 2 * width, WIDE), jnp.bfloat16),
            pltpu.VMEM((tiles, width, capacity), f32),
            pltpu.VMEM((tiles, width, capacity), f32),
            pltpu.VMEM((tiles, width, capacity // 2), f32),
            pltpu.VMEM((tiles, width, capacity // 2), f32),
            pltpu.VMEM((WIDE, 2 * (fields + 1) * groups), f32),
            pltpu.VMEM((2, levels, fields, lanes), f32),
            pltpu.VMEM((2, levels, fields, lanes), f32),
            pltpu.SemaphoreType.DMA((tiles,)),
            pltpu.SemaphoreType.DMA((tiles,)),
            pltpu.SemaphoreType.DMA((2,)),
            pltpu.SemaphoreType.DMA((2,)),
        ],
        compiler_params=pltpu.CompilerParams(
            collective_id=0, has_side_effects=True, vmem_limit_bytes=48 << 20
        ),
    )(
        pltpu.with_memory_space_constraint(mixing[0], pltpu.HBM),
        pltpu.with_memory_space_constraint(cell_counts[0, 0], pltpu.HBM), *held,
    )
    hbm = pl.BlockSpec(memory_space=pltpu.HBM)
    solved, surface = pl.pallas_call(
        finish,
        out_shape=(grid, jax.ShapeDtypeStruct((fields, rows, lanes), f32)),
        in_specs=[vmem, vmem, vmem],
        out_specs=(hbm, hbm),
        scratch_shapes=[
            pltpu.VMEM((levels, fields, rows, lanes), f32),
            pltpu.SemaphoreType.DMA((CHUNKS + 1,)),
        ],
        compiler_params=pltpu.CompilerParams(vmem_limit_bytes=8 << 20),
    )(base, slope, flux)
    return (solved[None], surface[None])


def solution(mesh):
    in_specs = (
        P("comp", None, None, "tile", None),
        P("comp", None, None, "tile", None),
        P("comp", None, "tile", None),
        P("comp", None, "tile", None),
        P("comp", "tile", None),
        P("comp", None),
        P("comp", "tile", None),
        P("comp", "tile", None, None),
        P("comp", "tile", None, None),
    )
    out_specs = (P("comp", None, None, "tile", None), P("comp", None, "tile", None))
    return jax.shard_map(
        on_device, mesh=mesh, in_specs=in_specs, out_specs=out_specs, check_vma=False
    )
```

```python
import functools

import jax
import jax.numpy as jnp
from jax import lax
from jax.experimental import pallas as pl
from jax.experimental.pallas import tpu as pltpu
from jax.sharding import PartitionSpec as P

MESH = pl.DeviceIdType.MESH
CHUNKS = 4
WIDE = 256
BATCH = 4


def split_two(values):
    high = values.astype(jnp.bfloat16).astype(jnp.float32)
    return high, values - high


def as_bf16(integers):
    return integers.astype(jnp.float32).astype(jnp.bfloat16)


def hot_of(cells, lanes, groups):
    row = cells // lanes
    group = row % groups
    inside = (row // groups) * lanes + cells % lanes
    place = as_bf16(lax.broadcasted_iota(jnp.int32, (WIDE, cells.shape[1]), 0))
    one, zero = jnp.ones((), jnp.bfloat16), jnp.zeros((), jnp.bfloat16)
    return jnp.where(place == as_bf16(inside), one, zero), group


def kernel(
    tiles,
    mixing_ref, counts_ref, tracers_hbm, diffusion_hbm, coupling_hbm, source_hbm, mask_hbm, cells_hbm, areas_hbm,
    base_ref, slope_ref, flux_ref,
    tracers_ref, diffusion_ref, coupling_ref, source_ref, mask_ref, cells_ref, areas_ref, load_sem,
    factor_ref, planes_ref, table_ref, table16_ref, own_ref, partner_ref, skin_ref, answer_ref, total_ref,
    edge_ref, halo_ref,
    send_sem, recv_sem, edge_send, edge_recv,
):
    levels, fields, rows, lanes = tracers_ref.shape
    capacity = cells_ref.shape[1]
    halves = WIDE // lanes
    groups = rows * lanes // WIDE
    width = 2 * fields
    dense = capacity // 2
    comp = lax.axis_index("comp")
    tile = lax.axis_index("tile")
    other = 1 - comp
    after = lax.rem(tile + 1, tiles)
    before = lax.rem(tile + tiles - 1, tiles)

    side = tiles // 2
    place_in_side = tile % side
    near_base = (tile // side) * side
    far_base = side - near_base

    def near_block(j):
        return near_base + (place_in_side + j) % side

    def asked_block(i):
        return far_base + (place_in_side + 1 + comp + 2 * i) % side

    def owned_block(i):
        return far_base + (place_in_side + side - 2 + comp - 2 * i) % side

    chunk = levels // CHUNKS

    def level_load(source, target, part, slot):
        span = pl.ds(part * chunk, chunk)
        return pltpu.make_async_copy(source.at[span], target.at[span], load_sem.at[slot])

    tracer_loads = [level_load(tracers_hbm, tracers_ref, c, c) for c in range(CHUNKS)]
    diffusion_loads = [level_load(diffusion_hbm, diffusion_ref, c, CHUNKS + c) for c in range(CHUNKS)]
    pairs = (
        (coupling_hbm, coupling_ref), (source_hbm, source_ref), (mask_hbm, mask_ref),
        (cells_hbm, cells_ref), (areas_hbm, areas_ref),
    )
    rest_loads = [
        pltpu.make_async_copy(held, target, load_sem.at[2 * CHUNKS + i]) for i, (held, target) in enumerate(pairs)
    ]
    for c in range(CHUNKS):
        diffusion_loads[c].start()
        if c >= 1:
            tracer_loads[c - 1].start()
    tracer_loads[CHUNKS - 1].start()
    for load in rest_loads:
        load.start()

    barrier = pltpu.get_barrier_semaphore()

    def greet(step, carry):
        pl.semaphore_signal(barrier, inc=1, device_id=(other, step), device_id_type=MESH)
        return carry

    lax.fori_loop(0, tiles, greet, 0)
    pl.semaphore_signal(barrier, inc=1, device_id=(comp, after), device_id_type=MESH)
    pl.semaphore_signal(barrier, inc=1, device_id=(comp, before), device_id_type=MESH)

    def down(k, carry):
        factor, reduced = carry
        here = diffusion_ref[k]
        below = diffusion_ref[k + 1]
        field = tracers_ref[k]
        inverse = 1.0 / (1.0 + here + below - here * factor)
        factor = below * inverse
        reduced = (field + here * reduced) * inverse
        factor_ref[k] = factor
        base_ref[k] = reduced
        edge_ref[0, k] = field[:, rows - 1, :]
        edge_ref[1, k] = field[:, 0, :]
        return factor, reduced

    zeros = jnp.zeros((fields, rows, lanes), jnp.float32)
    factor, reduced = zeros, zeros
    diffusion_loads[0].wait()
    for c in range(CHUNKS):
        if c + 1 < CHUNKS:
            diffusion_loads[c + 1].wait()
        tracer_loads[c].wait()
        end = min((c + 1) * chunk, levels - 1)
        factor, reduced = lax.fori_loop(c * chunk, end, down, (factor, reduced))
    for load in rest_loads:
        load.wait()
    last = levels - 1
    here = diffusion_ref[last]
    field = tracers_ref[last]
    admittance = 1.0 / (1.0 + here - here * factor)
    bottom = (field + here * reduced) * admittance
    edge_ref[0, last] = field[:, rows - 1, :]
    edge_ref[1, last] = field[:, 0, :]
    base_ref[last] = bottom
    slope_ref[last] = admittance
    mask = mask_ref[...].astype(jnp.float32)[None]
    coupling = coupling_ref[...]
    conductance = mask * coupling / (1.0 + coupling * admittance)
    offered = mask * (source_ref[...] + conductance * bottom)
    for k in range(width):
        plane = offered[k] if k < fields else conductance[k - fields]
        for half in range(halves):
            table_ref[half, pl.ds(k, groups, stride=width), :] = plane[half * groups : (half + 1) * groups]
    table = jnp.concatenate([table_ref[half] for half in range(halves)], axis=1)
    high, low = split_two(table.reshape(groups, width, WIDE))
    table16_ref[...] = (
        jnp.concatenate([high, low], axis=1).reshape(groups * 2 * width, WIDE).astype(jnp.bfloat16)
    )

    edge_up = pltpu.make_async_remote_copy(
        src_ref=edge_ref.at[0], dst_ref=halo_ref.at[0], send_sem=edge_send.at[0], recv_sem=edge_recv.at[0],
        device_id=(comp, after), device_id_type=MESH,
    )
    edge_down = pltpu.make_async_remote_copy(
        src_ref=edge_ref.at[1], dst_ref=halo_ref.at[1], send_sem=edge_send.at[1], recv_sem=edge_recv.at[1],
        device_id=(comp, before), device_id_type=MESH,
    )
    has_before, has_after = tile > 0, tile < tiles - 1

    def block_copy(block, slot):
        return pltpu.make_async_remote_copy(
            src_ref=own_ref.at[block], dst_ref=partner_ref.at[slot],
            send_sem=send_sem.at[block], recv_sem=recv_sem.at[slot],
            device_id=(other, block), device_id_type=MESH,
        )

    def answer_copy(block, slot):
        return pltpu.make_async_remote_copy(
            src_ref=skin_ref.at[block], dst_ref=answer_ref.at[slot],
            send_sem=send_sem.at[block], recv_sem=recv_sem.at[slot],
            device_id=(other, block), device_id_type=MESH,
        )

    def cells_of(block):
        return hot_of(cells_ref[pl.ds(block, 1), :], lanes, groups)

    def pick(blocks):
        hots, group = zip(*[cells_of(block) for block in blocks])
        found = jnp.dot(table16_ref[...], jnp.concatenate(hots, axis=1), preferred_element_type=jnp.float32)
        size = 2 * width
        chosen = [
            found[g * size : g * size + width] + found[g * size + width : (g + 1) * size] for g in range(groups)
        ]
        group = jnp.broadcast_to(jnp.concatenate(group, axis=1), (width, len(blocks) * capacity))
        stride = 1
        while len(chosen) > 1:
            odd = (group // stride) % 2 == 1
            chosen = [jnp.where(odd, chosen[i + 1], chosen[i]) for i in range(0, len(chosen), 2)]
            stride *= 2
        for i, block in enumerate(blocks):
            own_ref[block] = chosen[0][:, i * capacity : (i + 1) * capacity]

    def each(count, batch, block_of, do):
        def step(s, carry):
            do([block_of(s * batch + i) for i in range(batch)])
            return carry

        if count == batch:
            step(0, 0)
        else:
            lax.fori_loop(0, count // batch, step, 0)

    def pick_and_send(blocks):
        pick(blocks)
        for block in blocks:
            block_copy(block, tile).start()

    far_batch = min(BATCH, side // 2)
    near_batch = min(BATCH, side)

    each(side // 2, far_batch, asked_block, pick)

    pl.semaphore_wait(barrier, tiles + 2)

    def send(step, carry):
        block_copy(asked_block(step), tile).start()
        return carry

    lax.fori_loop(0, side // 2, send, 0)

    @pl.when(has_after)
    def _():
        edge_up.start()

    @pl.when(has_before)
    def _():
        edge_down.start()

    each(side // 2, far_batch, owned_block, pick)
    each(side, near_batch, near_block, pick_and_send)

    upper = lax.broadcasted_iota(jnp.int32, (width, dense), 0) < fields

    def skin_of(block):
        both = own_ref[block] + partner_ref[block]
        turned = pltpu.roll(both, fields, 0)
        offers = jnp.where(upper, both[:, :dense], turned[:, dense:])
        conducts = jnp.where(upper, turned[:, :dense], both[:, dense:])
        return offers / (conducts + 1.0)

    def answer(step, carry):
        block = owned_block(step)
        block_copy(block, block).wait_recv()
        skin_ref[block] = skin_of(block)
        answer_copy(block, tile).start()
        return carry

    lax.fori_loop(0, side // 2, answer, 0)

    @pl.when(has_after)
    def _():
        edge_up.wait_send()
        edge_down.wait_recv()

    @pl.when(has_before)
    def _():
        edge_down.wait_send()
        edge_up.wait_recv()

    @pl.when(tile == 0)
    def _():
        halo_ref[0] = jnp.zeros((levels, fields, lanes), jnp.float32)

    @pl.when(tile == tiles - 1)
    def _():
        halo_ref[1] = jnp.zeros((levels, fields, lanes), jnp.float32)

    row = lax.broadcasted_iota(jnp.int32, (fields, rows, lanes), 1)
    first_row = row == 0
    last_row = row == rows - 1
    which = lax.broadcasted_iota(jnp.int32, (fields, rows, lanes), 0)
    mix = jnp.zeros((fields, rows, lanes), jnp.float32)
    for f in range(fields):
        mix = jnp.where(which == f, mixing_ref[f], mix)

    def spread(k):
        field = tracers_ref[k]
        north = jnp.where(first_row, halo_ref[0, k][:, None, :], pltpu.roll(field, 1, 1))
        south = jnp.where(last_row, halo_ref[1, k][:, None, :], pltpu.roll(field, rows - 1, 1))
        along = pltpu.roll(field, 1, 2) + pltpu.roll(field, lanes - 1, 2)
        return mix * (north + south + along - 4.0 * field)

    base_ref[last] = bottom + spread(last)

    def up(step, carry):
        base, slope = carry
        k = levels - 2 - step
        factor = factor_ref[k]
        base = base_ref[k] + factor * base
        slope = factor * slope
        slope_ref[k] = slope
        base_ref[k] = base + spread(k)
        return base, slope

    lax.fori_loop(0, levels - 1, up, (bottom, admittance))

    total_ref[...] = jnp.zeros_like(total_ref)
    slot_of = lax.broadcasted_iota(jnp.int32, (1, capacity), 1)
    group_of = as_bf16(lax.broadcasted_iota(jnp.int32, (groups, capacity), 0))

    def scatter(blocks, skins):
        hots, lefts = [], []
        for block, skin in zip(blocks, skins):
            hot, group = cells_of(block)
            here = group_of == as_bf16(group)
            area = jnp.where(slot_of < counts_ref[block], areas_ref[pl.ds(block, 1), :], 0.0)
            weight = skin * jnp.where(upper, area[:, :dense], area[:, dense:])
            pieces = []
            for part, area_part in zip(split_two(weight), split_two(area)):
                found = [
                    jnp.concatenate([part[f : f + 1], part[fields + f : fields + f + 1]], axis=1)
                    for f in range(fields)
                ]
                for value in found + [area_part]:
                    spread_value = jnp.broadcast_to(value, (groups, capacity)).astype(jnp.bfloat16)
                    pieces.append(jnp.where(here, spread_value, jnp.zeros((), jnp.bfloat16)))
            hots.append(hot)
            lefts.append(jnp.concatenate(pieces, axis=0))
        total_ref[...] += lax.dot_general(
            jnp.concatenate(hots, axis=1), jnp.concatenate(lefts, axis=1), (((1,), (1,)), ((), ())),
            preferred_element_type=jnp.float32,
        )

    def scatter_owned(blocks):
        scatter(blocks, [skin_ref[block] for block in blocks])

    def scatter_near(blocks):
        for block in blocks:
            block_copy(block, block).wait_recv()
        scatter(blocks, [skin_of(block) for block in blocks])

    def scatter_asked(blocks):
        for block in blocks:
            answer_copy(block, block).wait_recv()
        scatter(blocks, [answer_ref[block] for block in blocks])

    each(side // 2, far_batch, owned_block, scatter_owned)
    each(side, near_batch, near_block, scatter_near)
    each(side // 2, 2, asked_block, scatter_asked)

    sums = (fields + 1) * groups
    totals = total_ref[...].T
    totals = totals[:sums] + totals[sums:]
    for k in range(fields + 1):
        for half in range(halves):
            planes_ref[k, half * groups : (half + 1) * groups, :] = totals[
                k * groups : (k + 1) * groups, half * lanes : (half + 1) * lanes
            ]
    flux_ref[...] = conductance * (planes_ref[0:fields] - bottom * planes_ref[fields : fields + 1])

    def drain(step, carry):
        block_copy(asked_block(step), tile).wait_send()
        answer_copy(owned_block(step), tile).wait_send()
        return carry

    def drain_near(step, carry):
        block_copy(near_block(step), tile).wait_send()
        return carry

    lax.fori_loop(0, side // 2, drain, 0)
    lax.fori_loop(0, side, drain_near, 0)


def finish(base_ref, slope_ref, flux_ref, solved_hbm, surface_hbm, solved_ref, store_sem):
    chunk = base_ref.shape[0] // CHUNKS
    flux_store = pltpu.make_async_copy(flux_ref, surface_hbm, store_sem.at[CHUNKS])
    flux_store.start()
    flux = flux_ref[...]
    stores = []
    for c in range(CHUNKS):
        span = pl.ds(c * chunk, chunk)

        def combine(k, carry):
            solved_ref[k] = base_ref[k] + slope_ref[k] * flux
            return carry

        lax.fori_loop(c * chunk, (c + 1) * chunk, combine, 0, unroll=True)
        stores.append(pltpu.make_async_copy(solved_ref.at[span], solved_hbm.at[span], store_sem.at[c]))
        stores[-1].start()
    flux_store.wait()
    for store in stores:
        store.wait()


def on_device(
    tracers, diffusion, coupling, source, sea_mask, mixing, cell_counts, cell_columns, cell_areas
):
    levels, fields, rows, lanes = tracers.shape[1:]
    tiles, capacity = cell_columns.shape[2:]
    width = 2 * fields
    groups = rows * lanes // WIDE
    f32 = jnp.float32
    grid = jax.ShapeDtypeStruct((levels, fields, rows, lanes), f32)
    vmem = pl.BlockSpec(memory_space=pltpu.VMEM)
    smem = pl.BlockSpec(memory_space=pltpu.SMEM)
    held = [
        pltpu.with_memory_space_constraint(array, pltpu.HBM)
        for array in (
            tracers[0], diffusion[0], coupling[0], source[0], sea_mask[0], cell_columns[0, 0], cell_areas[0, 0]
        )
    ]
    base, slope, flux = pl.pallas_call(
        functools.partial(kernel, tiles),
        out_shape=(grid, grid, jax.ShapeDtypeStruct((fields, rows, lanes), f32)),
        in_specs=[smem, smem] + [pl.BlockSpec(memory_space=pltpu.HBM)] * 7,
        out_specs=(vmem, vmem, vmem),
        scratch_shapes=[
            pltpu.VMEM((levels, fields, rows, lanes), f32),
            pltpu.VMEM((levels, fields, rows, lanes), f32),
            pltpu.VMEM((fields, rows, lanes), f32),
            pltpu.VMEM((fields, rows, lanes), f32),
            pltpu.VMEM((rows, lanes), jnp.int32),
            pltpu.VMEM((tiles, capacity), jnp.int32),
            pltpu.VMEM((tiles, capacity), f32),
            pltpu.SemaphoreType.DMA((2 * CHUNKS + 5,)),
            pltpu.VMEM((levels, fields, rows, lanes), f32),
            pltpu.VMEM((fields + 1, rows, lanes), f32),
            pltpu.VMEM((WIDE // lanes, groups * width, lanes), f32),
            pltpu.VMEM((groups * 2 * width, WIDE), jnp.bfloat16),
            pltpu.VMEM((tiles, width, capacity), f32),
            pltpu.VMEM((tiles, width, capacity), f32),
            pltpu.VMEM((tiles, width, capacity // 2), f32),
            pltpu.VMEM((tiles, width, capacity // 2), f32),
            pltpu.VMEM((WIDE, 2 * (fields + 1) * groups), f32),
            pltpu.VMEM((2, levels, fields, lanes), f32),
            pltpu.VMEM((2, levels, fields, lanes), f32),
            pltpu.SemaphoreType.DMA((tiles,)),
            pltpu.SemaphoreType.DMA((tiles,)),
            pltpu.SemaphoreType.DMA((2,)),
            pltpu.SemaphoreType.DMA((2,)),
        ],
        compiler_params=pltpu.CompilerParams(
            collective_id=0, has_side_effects=True, vmem_limit_bytes=48 << 20
        ),
    )(
        pltpu.with_memory_space_constraint(mixing[0], pltpu.HBM),
        pltpu.with_memory_space_constraint(cell_counts[0, 0], pltpu.HBM), *held,
    )
    hbm = pl.BlockSpec(memory_space=pltpu.HBM)
    solved, surface = pl.pallas_call(
        finish,
        out_shape=(grid, jax.ShapeDtypeStruct((fields, rows, lanes), f32)),
        in_specs=[vmem, vmem, vmem],
        out_specs=(hbm, hbm),
        scratch_shapes=[
            pltpu.VMEM((levels, fields, rows, lanes), f32),
            pltpu.SemaphoreType.DMA((CHUNKS + 1,)),
        ],
        compiler_params=pltpu.CompilerParams(vmem_limit_bytes=8 << 20),
    )(base, slope, flux)
    return (solved[None], surface[None])


def solution(mesh):
    in_specs = (
        P("comp", None, None, "tile", None),
        P("comp", None, None, "tile", None),
        P("comp", None, "tile", None),
        P("comp", None, "tile", None),
        P("comp", "tile", None),
        P("comp", None),
        P("comp", "tile", None),
        P("comp", "tile", None, None),
        P("comp", "tile", None, None),
    )
    out_specs = (P("comp", None, None, "tile", None), P("comp", None, "tile", None))
    return jax.shard_map(
        on_device, mesh=mesh, in_specs=in_specs, out_specs=out_specs, check_vma=False
    )
```

```python
import functools

import jax
import jax.numpy as jnp
from jax import lax
from jax.experimental import pallas as pl
from jax.experimental.pallas import tpu as pltpu
from jax.sharding import PartitionSpec as P

MESH = pl.DeviceIdType.MESH
CHUNKS = 4
WIDE = 256
BATCH = 4


def split_two(values):
    high = values.astype(jnp.bfloat16).astype(jnp.float32)
    return high, values - high


def as_bf16(integers):
    return integers.astype(jnp.float32).astype(jnp.bfloat16)


def hot_of(cells, lanes, groups):
    row = cells // lanes
    group = row % groups
    inside = (row // groups) * lanes + cells % lanes
    place = as_bf16(lax.broadcasted_iota(jnp.int32, (WIDE, cells.shape[1]), 0))
    one, zero = jnp.ones((), jnp.bfloat16), jnp.zeros((), jnp.bfloat16)
    return jnp.where(place == as_bf16(inside), one, zero), group


def kernel(
    tiles,
    mixing_hbm, counts_hbm, tracers_hbm, diffusion_hbm, coupling_hbm, source_hbm, mask_hbm, cells_hbm, areas_hbm,
    base_ref, slope_ref, flux_ref,
    tracers_ref, diffusion_ref, coupling_ref, source_ref, mask_ref, cells_ref, areas_ref, mixing_ref, counts_ref,
    load_sem,
    factor_ref, planes_ref, table_ref, table16_ref, own_ref, partner_ref, skin_ref, answer_ref, total_ref,
    edge_ref, halo_ref,
    send_sem, recv_sem, edge_send, edge_recv,
):
    levels, fields, rows, lanes = tracers_ref.shape
    capacity = cells_ref.shape[1]
    halves = WIDE // lanes
    groups = rows * lanes // WIDE
    width = 2 * fields
    dense = capacity // 2
    comp = lax.axis_index("comp")
    tile = lax.axis_index("tile")
    other = 1 - comp
    after = lax.rem(tile + 1, tiles)
    before = lax.rem(tile + tiles - 1, tiles)

    side = tiles // 2
    place_in_side = tile % side
    near_base = (tile // side) * side
    far_base = side - near_base

    def near_block(j):
        return near_base + (place_in_side + j) % (side // 2) + (j // (side // 2)) * (side // 2)

    def in_order(odd, i):
        part = side // 4
        return odd + 2 * ((i + place_in_side // 2) % part) + (i // part) * (side // 2)

    def asked_block(i):
        return far_base + in_order((place_in_side + 1 + comp) % 2, i)

    def owned_block(i):
        return far_base + in_order((place_in_side + comp) % 2, i)

    chunk = levels // CHUNKS

    def level_load(source, target, part, slot):
        span = pl.ds(part * chunk, chunk)
        return pltpu.make_async_copy(source.at[span], target.at[span], load_sem.at[slot])

    tracer_loads = [level_load(tracers_hbm, tracers_ref, c, c) for c in range(CHUNKS)]
    diffusion_loads = [level_load(diffusion_hbm, diffusion_ref, c, CHUNKS + c) for c in range(CHUNKS)]
    pairs = (
        (coupling_hbm, coupling_ref), (source_hbm, source_ref), (mask_hbm, mask_ref),
        (cells_hbm, cells_ref), (areas_hbm, areas_ref), (mixing_hbm, mixing_ref), (counts_hbm, counts_ref),
    )
    rest_loads = [
        pltpu.make_async_copy(held, target, load_sem.at[2 * CHUNKS + i]) for i, (held, target) in enumerate(pairs)
    ]
    for c in range(CHUNKS):
        diffusion_loads[c].start()
        if c >= 1:
            tracer_loads[c - 1].start()
    tracer_loads[CHUNKS - 1].start()
    for load in rest_loads:
        load.start()

    barrier = pltpu.get_barrier_semaphore()

    def greet(step, carry):
        pl.semaphore_signal(barrier, inc=1, device_id=(other, step), device_id_type=MESH)
        return carry

    lax.fori_loop(0, tiles, greet, 0)
    pl.semaphore_signal(barrier, inc=1, device_id=(comp, after), device_id_type=MESH)
    pl.semaphore_signal(barrier, inc=1, device_id=(comp, before), device_id_type=MESH)

    def down(k, carry):
        factor, reduced = carry
        here = diffusion_ref[k]
        below = diffusion_ref[k + 1]
        field = tracers_ref[k]
        inverse = 1.0 / (1.0 + here + below - here * factor)
        factor = below * inverse
        reduced = (field + here * reduced) * inverse
        factor_ref[k] = factor
        base_ref[k] = reduced
        edge_ref[0, k] = field[:, rows - 1, :]
        edge_ref[1, k] = field[:, 0, :]
        return factor, reduced

    zeros = jnp.zeros((fields, rows, lanes), jnp.float32)
    factor, reduced = zeros, zeros
    diffusion_loads[0].wait()
    for c in range(CHUNKS):
        if c + 1 < CHUNKS:
            diffusion_loads[c + 1].wait()
        tracer_loads[c].wait()
        end = min((c + 1) * chunk, levels - 1)
        factor, reduced = lax.fori_loop(c * chunk, end, down, (factor, reduced))
    for load in rest_loads:
        load.wait()
    last = levels - 1
    here = diffusion_ref[last]
    field = tracers_ref[last]
    admittance = 1.0 / (1.0 + here - here * factor)
    bottom = (field + here * reduced) * admittance
    edge_ref[0, last] = field[:, rows - 1, :]
    edge_ref[1, last] = field[:, 0, :]
    base_ref[last] = bottom
    slope_ref[last] = admittance
    mask = mask_ref[...].astype(jnp.float32)[None]
    coupling = coupling_ref[...]
    conductance = mask * coupling / (1.0 + coupling * admittance)
    offered = mask * (source_ref[...] + conductance * bottom)
    for k in range(width):
        plane = offered[k] if k < fields else conductance[k - fields]
        for half in range(halves):
            table_ref[half, pl.ds(k, groups, stride=width), :] = plane[half * groups : (half + 1) * groups]
    table = jnp.concatenate([table_ref[half] for half in range(halves)], axis=1)
    high, low = split_two(table.reshape(groups, width, WIDE))
    table16_ref[...] = (
        jnp.concatenate([high, low], axis=1).reshape(groups * 2 * width, WIDE).astype(jnp.bfloat16)
    )

    edge_up = pltpu.make_async_remote_copy(
        src_ref=edge_ref.at[0], dst_ref=halo_ref.at[0], send_sem=edge_send.at[0], recv_sem=edge_recv.at[0],
        device_id=(comp, after), device_id_type=MESH,
    )
    edge_down = pltpu.make_async_remote_copy(
        src_ref=edge_ref.at[1], dst_ref=halo_ref.at[1], send_sem=edge_send.at[1], recv_sem=edge_recv.at[1],
        device_id=(comp, before), device_id_type=MESH,
    )
    has_before, has_after = tile > 0, tile < tiles - 1

    def block_copy(block, slot):
        return pltpu.make_async_remote_copy(
            src_ref=own_ref.at[block], dst_ref=partner_ref.at[slot],
            send_sem=send_sem.at[block], recv_sem=recv_sem.at[slot],
            device_id=(other, block), device_id_type=MESH,
        )

    def answer_copy(block, slot):
        return pltpu.make_async_remote_copy(
            src_ref=skin_ref.at[block], dst_ref=answer_ref.at[slot],
            send_sem=send_sem.at[block], recv_sem=recv_sem.at[slot],
            device_id=(other, block), device_id_type=MESH,
        )

    def cells_of(block):
        return hot_of(cells_ref[pl.ds(block, 1), :], lanes, groups)

    def pick(blocks):
        hots, group = zip(*[cells_of(block) for block in blocks])
        found = jnp.dot(table16_ref[...], jnp.concatenate(hots, axis=1), preferred_element_type=jnp.float32)
        size = 2 * width
        chosen = [
            found[g * size : g * size + width] + found[g * size + width : (g + 1) * size] for g in range(groups)
        ]
        group = jnp.broadcast_to(jnp.concatenate(group, axis=1), (width, len(blocks) * capacity))
        stride = 1
        while len(chosen) > 1:
            odd = (group // stride) % 2 == 1
            chosen = [jnp.where(odd, chosen[i + 1], chosen[i]) for i in range(0, len(chosen), 2)]
            stride *= 2
        for i, block in enumerate(blocks):
            own_ref[block] = chosen[0][:, i * capacity : (i + 1) * capacity]

    def each(count, batch, block_of, do):
        def step(s, carry):
            do([block_of(s * batch + i) for i in range(batch)])
            return carry

        if count == batch:
            step(0, 0)
        else:
            lax.fori_loop(0, count // batch, step, 0)

    def pick_and_send(blocks):
        pick(blocks)
        for block in blocks:
            block_copy(block, tile).start()

    far_batch = min(BATCH, side // 2)
    near_batch = min(BATCH, side)

    each(side // 2, far_batch, asked_block, pick)

    pl.semaphore_wait(barrier, tiles + 2)

    @pl.when(has_after)
    def _():
        edge_up.start()

    @pl.when(has_before)
    def _():
        edge_down.start()

    def send(step, carry):
        block_copy(asked_block(step), tile).start()
        return carry

    lax.fori_loop(0, side // 2, send, 0)

    each(side // 2, far_batch, owned_block, pick)
    each(side, near_batch, near_block, pick_and_send)

    upper = lax.broadcasted_iota(jnp.int32, (width, dense), 0) < fields

    def skin_of(block):
        both = own_ref[block] + partner_ref[block]
        turned = pltpu.roll(both, fields, 0)
        offers = jnp.where(upper, both[:, :dense], turned[:, dense:])
        conducts = jnp.where(upper, turned[:, :dense], both[:, dense:])
        return offers / (conducts + 1.0)

    def answer(step, carry):
        block = owned_block(step)
        block_copy(block, block).wait_recv()
        skin_ref[block] = skin_of(block)
        answer_copy(block, tile).start()
        return carry

    def rise():
        @pl.when(has_after)
        def _():
            edge_up.wait_send()
            edge_down.wait_recv()

        @pl.when(has_before)
        def _():
            edge_down.wait_send()
            edge_up.wait_recv()

        @pl.when(tile == 0)
        def _():
            halo_ref[0] = jnp.zeros((levels, fields, lanes), jnp.float32)

        @pl.when(tile == tiles - 1)
        def _():
            halo_ref[1] = jnp.zeros((levels, fields, lanes), jnp.float32)

        row = lax.broadcasted_iota(jnp.int32, (fields, rows, lanes), 1)
        first_row = row == 0
        last_row = row == rows - 1
        which = lax.broadcasted_iota(jnp.int32, (fields, rows, lanes), 0)
        mix = jnp.zeros((fields, rows, lanes), jnp.float32)
        for f in range(fields):
            mix = jnp.where(which == f, mixing_ref[f], mix)

        def spread(k):
            field = tracers_ref[k]
            north = jnp.where(first_row, halo_ref[0, k][:, None, :], pltpu.roll(field, 1, 1))
            south = jnp.where(last_row, halo_ref[1, k][:, None, :], pltpu.roll(field, rows - 1, 1))
            along = pltpu.roll(field, 1, 2) + pltpu.roll(field, lanes - 1, 2)
            return mix * (north + south + along - 4.0 * field)

        base_ref[last] = bottom + spread(last)

        def up(step, carry):
            base, slope = carry
            k = levels - 2 - step
            factor = factor_ref[k]
            base = base_ref[k] + factor * base
            slope = factor * slope
            slope_ref[k] = slope
            base_ref[k] = base + spread(k)
            return base, slope

        lax.fori_loop(0, levels - 1, up, (bottom, admittance))

    early = tile < side

    @pl.when(early)
    def _():
        rise()

    lax.fori_loop(0, side // 2, answer, 0)

    @pl.when(jnp.logical_not(early))
    def _():
        rise()


    total_ref[...] = jnp.zeros_like(total_ref)
    slot_of = lax.broadcasted_iota(jnp.int32, (1, capacity), 1)
    group_of = as_bf16(lax.broadcasted_iota(jnp.int32, (groups, capacity), 0))

    def scatter(blocks, skins):
        hots, lefts = [], []
        for block, skin in zip(blocks, skins):
            hot, group = cells_of(block)
            here = group_of == as_bf16(group)
            area = jnp.where(slot_of < counts_ref[block], areas_ref[pl.ds(block, 1), :], 0.0)
            weight = skin * jnp.where(upper, area[:, :dense], area[:, dense:])
            pieces = []
            for part, area_part in zip(split_two(weight), split_two(area)):
                found = [
                    jnp.concatenate([part[f : f + 1], part[fields + f : fields + f + 1]], axis=1)
                    for f in range(fields)
                ]
                for value in found + [area_part]:
                    spread_value = jnp.broadcast_to(value, (groups, capacity)).astype(jnp.bfloat16)
                    pieces.append(jnp.where(here, spread_value, jnp.zeros((), jnp.bfloat16)))
            hots.append(hot)
            lefts.append(jnp.concatenate(pieces, axis=0))
        total_ref[...] += lax.dot_general(
            jnp.concatenate(hots, axis=1), jnp.concatenate(lefts, axis=1), (((1,), (1,)), ((), ())),
            preferred_element_type=jnp.float32,
        )

    def scatter_owned(blocks):
        scatter(blocks, [skin_ref[block] for block in blocks])

    def scatter_near(blocks):
        for block in blocks:
            block_copy(block, block).wait_recv()
        scatter(blocks, [skin_of(block) for block in blocks])

    def scatter_asked(blocks):
        for block in blocks:
            answer_copy(block, block).wait_recv()
        scatter(blocks, [answer_ref[block] for block in blocks])

    each(side // 2, far_batch, owned_block, scatter_owned)
    each(side, near_batch, near_block, scatter_near)
    each(side // 2, 2, asked_block, scatter_asked)

    sums = (fields + 1) * groups
    totals = total_ref[...].T
    totals = totals[:sums] + totals[sums:]
    for k in range(fields + 1):
        for half in range(halves):
            planes_ref[k, half * groups : (half + 1) * groups, :] = totals[
                k * groups : (k + 1) * groups, half * lanes : (half + 1) * lanes
            ]
    flux_ref[...] = conductance * (planes_ref[0:fields] - bottom * planes_ref[fields : fields + 1])

    def drain(step, carry):
        block_copy(asked_block(step), tile).wait_send()
        answer_copy(owned_block(step), tile).wait_send()
        return carry

    def drain_near(step, carry):
        block_copy(near_block(step), tile).wait_send()
        return carry

    lax.fori_loop(0, side // 2, drain, 0)
    lax.fori_loop(0, side, drain_near, 0)


def finish(base_ref, slope_ref, flux_ref, solved_hbm, surface_hbm, solved_ref, store_sem):
    chunk = base_ref.shape[0] // CHUNKS
    flux_store = pltpu.make_async_copy(flux_ref, surface_hbm, store_sem.at[CHUNKS])
    flux_store.start()
    flux = flux_ref[...]
    stores = []
    for c in range(CHUNKS):
        span = pl.ds(c * chunk, chunk)

        def combine(k, carry):
            solved_ref[k] = base_ref[k] + slope_ref[k] * flux
            return carry

        lax.fori_loop(c * chunk, (c + 1) * chunk, combine, 0, unroll=True)
        stores.append(pltpu.make_async_copy(solved_ref.at[span], solved_hbm.at[span], store_sem.at[c]))
        stores[-1].start()
    flux_store.wait()
    for store in stores:
        store.wait()


def on_device(
    tracers, diffusion, coupling, source, sea_mask, mixing, cell_counts, cell_columns, cell_areas
):
    levels, fields, rows, lanes = tracers.shape[1:]
    tiles, capacity = cell_columns.shape[2:]
    width = 2 * fields
    groups = rows * lanes // WIDE
    f32 = jnp.float32
    grid = jax.ShapeDtypeStruct((levels, fields, rows, lanes), f32)
    vmem = pl.BlockSpec(memory_space=pltpu.VMEM)
    held = [
        pltpu.with_memory_space_constraint(array, pltpu.HBM)
        for array in (
            tracers[0], diffusion[0], coupling[0], source[0], sea_mask[0], cell_columns[0, 0], cell_areas[0, 0]
        )
    ]
    base, slope, flux = pl.pallas_call(
        functools.partial(kernel, tiles),
        out_shape=(grid, grid, jax.ShapeDtypeStruct((fields, rows, lanes), f32)),
        in_specs=[pl.BlockSpec(memory_space=pltpu.HBM)] * 9,
        out_specs=(vmem, vmem, vmem),
        scratch_shapes=[
            pltpu.VMEM((levels, fields, rows, lanes), f32),
            pltpu.VMEM((levels, fields, rows, lanes), f32),
            pltpu.VMEM((fields, rows, lanes), f32),
            pltpu.VMEM((fields, rows, lanes), f32),
            pltpu.VMEM((rows, lanes), jnp.int32),
            pltpu.VMEM((tiles, capacity), jnp.int32),
            pltpu.VMEM((tiles, capacity), f32),
            pltpu.SMEM((fields,), f32),
            pltpu.SMEM((tiles,), jnp.int32),
            pltpu.SemaphoreType.DMA((2 * CHUNKS + 7,)),
            pltpu.VMEM((levels, fields, rows, lanes), f32),
            pltpu.VMEM((fields + 1, rows, lanes), f32),
            pltpu.VMEM((WIDE // lanes, groups * width, lanes), f32),
            pltpu.VMEM((groups * 2 * width, WIDE), jnp.bfloat16),
            pltpu.VMEM((tiles, width, capacity), f32),
            pltpu.VMEM((tiles, width, capacity), f32),
            pltpu.VMEM((tiles, width, capacity // 2), f32),
            pltpu.VMEM((tiles, width, capacity // 2), f32),
            pltpu.VMEM((WIDE, 2 * (fields + 1) * groups), f32),
            pltpu.VMEM((2, levels, fields, lanes), f32),
            pltpu.VMEM((2, levels, fields, lanes), f32),
            pltpu.SemaphoreType.DMA((tiles,)),
            pltpu.SemaphoreType.DMA((tiles,)),
            pltpu.SemaphoreType.DMA((2,)),
            pltpu.SemaphoreType.DMA((2,)),
        ],
        compiler_params=pltpu.CompilerParams(
            collective_id=0, has_side_effects=True, vmem_limit_bytes=48 << 20
        ),
    )(
        pltpu.with_memory_space_constraint(mixing[0], pltpu.HBM),
        pltpu.with_memory_space_constraint(cell_counts[0, 0], pltpu.HBM), *held,
    )
    hbm = pl.BlockSpec(memory_space=pltpu.HBM)
    solved, surface = pl.pallas_call(
        finish,
        out_shape=(grid, jax.ShapeDtypeStruct((fields, rows, lanes), f32)),
        in_specs=[vmem, vmem, vmem],
        out_specs=(hbm, hbm),
        scratch_shapes=[
            pltpu.VMEM((levels, fields, rows, lanes), f32),
            pltpu.SemaphoreType.DMA((CHUNKS + 1,)),
        ],
        compiler_params=pltpu.CompilerParams(vmem_limit_bytes=8 << 20),
    )(base, slope, flux)
    return (solved[None], surface[None])


def solution(mesh):
    in_specs = (
        P("comp", None, None, "tile", None),
        P("comp", None, None, "tile", None),
        P("comp", None, "tile", None),
        P("comp", None, "tile", None),
        P("comp", "tile", None),
        P("comp", None),
        P("comp", "tile", None),
        P("comp", "tile", None, None),
        P("comp", "tile", None, None),
    )
    out_specs = (P("comp", None, None, "tile", None), P("comp", None, "tile", None))
    return jax.shard_map(
        on_device, mesh=mesh, in_specs=in_specs, out_specs=out_specs, check_vma=False
    )
```

```python
import functools

import jax
import jax.numpy as jnp
from jax import lax
from jax.experimental import pallas as pl
from jax.experimental.pallas import tpu as pltpu
from jax.sharding import PartitionSpec as P

MESH = pl.DeviceIdType.MESH
CHUNKS = 4
WIDE = 256
BATCH = 4


def split_two(values):
    high = values.astype(jnp.bfloat16).astype(jnp.float32)
    return high, values - high


def as_bf16(integers):
    return integers.astype(jnp.float32).astype(jnp.bfloat16)


def hot_of(cells, lanes, groups):
    row = cells // lanes
    group = row % groups
    inside = (row // groups) * lanes + cells % lanes
    place = as_bf16(lax.broadcasted_iota(jnp.int32, (WIDE, cells.shape[1]), 0))
    one, zero = jnp.ones((), jnp.bfloat16), jnp.zeros((), jnp.bfloat16)
    return jnp.where(place == as_bf16(inside), one, zero), group


def kernel(
    tiles,
    mixing_hbm, counts_hbm, tracers_hbm, diffusion_hbm, coupling_hbm, source_hbm, mask_hbm, cells_hbm, areas_hbm,
    base_ref, slope_ref, flux_ref,
    tracers_ref, diffusion_ref, coupling_ref, source_ref, mask_ref, cells_ref, areas_ref, mixing_ref, counts_ref,
    load_sem,
    factor_ref, planes_ref, table_ref, table16_ref, own_ref, partner_ref, skin_ref, answer_ref, total_ref,
    edge_ref, halo_ref,
    send_sem, recv_sem, edge_send, edge_recv, word_sem,
):
    levels, fields, rows, lanes = tracers_ref.shape
    capacity = cells_ref.shape[1]
    halves = WIDE // lanes
    groups = rows * lanes // WIDE
    width = 2 * fields
    dense = capacity // 2
    comp = lax.axis_index("comp")
    tile = lax.axis_index("tile")
    other = 1 - comp
    after = lax.rem(tile + 1, tiles)
    before = lax.rem(tile + tiles - 1, tiles)

    side = tiles // 2
    place_in_side = tile % side
    near_base = (tile // side) * side
    far_base = side - near_base

    def near_block(j):
        return near_base + (place_in_side + j) % (side // 2) + (j // (side // 2)) * (side // 2)

    def in_order(first, i):
        part = side // 4
        return (place_in_side + first + 2 * (i % part)) % (2 * part) + (i // part) * 2 * part

    def asked_block(i):
        return far_base + in_order(comp, i)

    def owned_block(i):
        return far_base + in_order(1 - comp, i)

    chunk = levels // CHUNKS

    def level_load(source, target, part, slot):
        span = pl.ds(part * chunk, chunk)
        return pltpu.make_async_copy(source.at[span], target.at[span], load_sem.at[slot])

    tracer_loads = [level_load(tracers_hbm, tracers_ref, c, c) for c in range(CHUNKS)]
    diffusion_loads = [level_load(diffusion_hbm, diffusion_ref, c, CHUNKS + c) for c in range(CHUNKS)]
    pairs = (
        (coupling_hbm, coupling_ref), (source_hbm, source_ref), (mask_hbm, mask_ref),
        (cells_hbm, cells_ref), (areas_hbm, areas_ref), (mixing_hbm, mixing_ref), (counts_hbm, counts_ref),
    )
    rest_loads = [
        pltpu.make_async_copy(held, target, load_sem.at[2 * CHUNKS + i]) for i, (held, target) in enumerate(pairs)
    ]
    for c in range(CHUNKS):
        diffusion_loads[c].start()
        if c >= 1:
            tracer_loads[c - 1].start()
    tracer_loads[CHUNKS - 1].start()
    for load in rest_loads:
        load.start()

    barrier = pltpu.get_barrier_semaphore()

    most = tiles - tiles // 4
    late = tile >= most
    prompt = tile < most
    has_before, has_after = tile > 0, tile < tiles - 1
    is_seam_low, is_seam_high = tile == most - 1, tile == most

    def greet(device_comp, block):
        pl.semaphore_signal(barrier, inc=1, device_id=(device_comp, block), device_id_type=MESH)

    def greet_all(device_comp, first, end):
        def step(block, carry):
            greet(device_comp, block)
            return carry

        lax.fori_loop(first, end, step, 0)

    @pl.when(prompt)
    def _():
        @pl.when(comp == 1)
        def _():
            greet_all(1, 0, tile)
            greet_all(1, tile + 1, most)

        @pl.when(comp == 0)
        def _():
            greet_all(1, 0, most)

        greet_all(other, most, tiles)

    @pl.when(late)
    def _():
        greet_all(0, 0, most)
        greet_all(other, most, tiles)

    @pl.when(jnp.logical_and(late, jnp.logical_not(is_seam_high)))
    def _():
        greet(comp, before)

    @pl.when(jnp.logical_and(tile >= most - 1, has_after))
    def _():
        greet(comp, after)

    def down(k, carry):
        factor, reduced = carry
        here = diffusion_ref[k]
        below = diffusion_ref[k + 1]
        field = tracers_ref[k]
        inverse = 1.0 / (1.0 + here + below - here * factor)
        factor = below * inverse
        reduced = (field + here * reduced) * inverse
        factor_ref[k] = factor
        base_ref[k] = reduced
        edge_ref[0, k] = field[:, rows - 1, :]
        edge_ref[1, k] = field[:, 0, :]
        return factor, reduced

    zeros = jnp.zeros((fields, rows, lanes), jnp.float32)
    factor, reduced = zeros, zeros
    diffusion_loads[0].wait()
    for c in range(CHUNKS):
        if c + 1 < CHUNKS:
            diffusion_loads[c + 1].wait()
        tracer_loads[c].wait()
        end = min((c + 1) * chunk, levels - 1)
        factor, reduced = lax.fori_loop(c * chunk, end, down, (factor, reduced))
    for load in rest_loads:
        load.wait()
    last = levels - 1
    here = diffusion_ref[last]
    field = tracers_ref[last]
    admittance = 1.0 / (1.0 + here - here * factor)
    bottom = (field + here * reduced) * admittance
    edge_ref[0, last] = field[:, rows - 1, :]
    edge_ref[1, last] = field[:, 0, :]
    base_ref[last] = bottom
    slope_ref[last] = admittance
    mask = mask_ref[...].astype(jnp.float32)[None]
    coupling = coupling_ref[...]
    conductance = mask * coupling / (1.0 + coupling * admittance)
    offered = mask * (source_ref[...] + conductance * bottom)
    for k in range(width):
        plane = offered[k] if k < fields else conductance[k - fields]
        for half in range(halves):
            table_ref[half, pl.ds(k, groups, stride=width), :] = plane[half * groups : (half + 1) * groups]
    table = jnp.concatenate([table_ref[half] for half in range(halves)], axis=1)
    high, low = split_two(table.reshape(groups, width, WIDE))
    table16_ref[...] = (
        jnp.concatenate([high, low], axis=1).reshape(groups * 2 * width, WIDE).astype(jnp.bfloat16)
    )

    edge_up = pltpu.make_async_remote_copy(
        src_ref=edge_ref.at[0], dst_ref=halo_ref.at[0], send_sem=edge_send.at[0], recv_sem=edge_recv.at[0],
        device_id=(comp, after), device_id_type=MESH,
    )
    edge_down = pltpu.make_async_remote_copy(
        src_ref=edge_ref.at[1], dst_ref=halo_ref.at[1], send_sem=edge_send.at[1], recv_sem=edge_recv.at[1],
        device_id=(comp, before), device_id_type=MESH,
    )
    def block_copy(block, slot):
        return pltpu.make_async_remote_copy(
            src_ref=own_ref.at[block], dst_ref=partner_ref.at[slot],
            send_sem=send_sem.at[block], recv_sem=recv_sem.at[slot],
            device_id=(other, block), device_id_type=MESH,
        )

    def answer_copy(block, slot):
        return pltpu.make_async_remote_copy(
            src_ref=skin_ref.at[block], dst_ref=answer_ref.at[slot],
            send_sem=send_sem.at[block], recv_sem=recv_sem.at[slot],
            device_id=(other, block), device_id_type=MESH,
        )

    def cells_of(block):
        return hot_of(cells_ref[pl.ds(block, 1), :], lanes, groups)

    def pick(blocks):
        hots, group = zip(*[cells_of(block) for block in blocks])
        found = jnp.dot(table16_ref[...], jnp.concatenate(hots, axis=1), preferred_element_type=jnp.float32)
        size = 2 * width
        chosen = [
            found[g * size : g * size + width] + found[g * size + width : (g + 1) * size] for g in range(groups)
        ]
        group = jnp.broadcast_to(jnp.concatenate(group, axis=1), (width, len(blocks) * capacity))
        stride = 1
        while len(chosen) > 1:
            odd = (group // stride) % 2 == 1
            chosen = [jnp.where(odd, chosen[i + 1], chosen[i]) for i in range(0, len(chosen), 2)]
            stride *= 2
        for i, block in enumerate(blocks):
            own_ref[block] = chosen[0][:, i * capacity : (i + 1) * capacity]

    def each(count, batch, block_of, do, first=0):
        def step(s, carry):
            do([block_of(first + s * batch + i) for i in range(batch)])
            return carry

        if count == batch:
            step(0, 0)
        else:
            lax.fori_loop(0, count // batch, step, 0)

    def pick_and_send(blocks):
        pick(blocks)
        for block in blocks:
            block_copy(block, tile).start()

    far_batch = min(BATCH, side // 2)
    near_batch = min(BATCH, side)
    near_half = min(BATCH, side // 2)

    each(side // 2, far_batch, asked_block, pick)

    def one_unless_zero(number):
        return (number + tiles - 1) // tiles

    @pl.when(jnp.logical_and(prompt, comp == 1))
    def _():
        pl.semaphore_wait(barrier, 2 * most - 1)
        pl.semaphore_signal(word_sem, inc=1, device_id=(other, tile), device_id_type=MESH)

    @pl.when(jnp.logical_and(prompt, comp == 0))
    def _():
        pl.semaphore_wait(word_sem, 1)

    @pl.when(late)
    def _():
        pl.semaphore_wait(barrier, tiles + 1 + one_unless_zero(tiles - 1 - tile))

    @pl.when(jnp.logical_and(has_after, jnp.logical_not(is_seam_low)))
    def _():
        edge_up.start()

    @pl.when(has_before)
    def _():
        edge_down.start()

    def send(step, carry):
        block_copy(asked_block(step), tile).start()
        return carry

    early = tile < side
    part = side // 4
    lax.fori_loop(0, part, send, 0)

    @pl.when(jnp.logical_not(early))
    def _():
        lax.fori_loop(part, 2 * part, send, 0)

    each(side // 2, near_half, near_block, pick_and_send)

    @pl.when(jnp.logical_and(prompt, comp == 0))
    def _():
        pl.semaphore_wait(barrier, 2 * (tiles - most))
        pl.semaphore_signal(word_sem, inc=1, device_id=(other, tile), device_id_type=MESH)

    @pl.when(jnp.logical_and(prompt, comp == 1))
    def _():
        pl.semaphore_wait(word_sem, 1)

    @pl.when(is_seam_low)
    def _():
        edge_up.start()

    @pl.when(early)
    def _():
        lax.fori_loop(part, 2 * part, send, 0)

    each(side // 2, far_batch, owned_block, pick)
    each(side // 2, near_half, near_block, pick_and_send, first=side // 2)

    upper = lax.broadcasted_iota(jnp.int32, (width, dense), 0) < fields

    def skin_of(block):
        both = own_ref[block] + partner_ref[block]
        turned = pltpu.roll(both, fields, 0)
        offers = jnp.where(upper, both[:, :dense], turned[:, dense:])
        conducts = jnp.where(upper, turned[:, :dense], both[:, dense:])
        return offers / (conducts + 1.0)

    def answer(step, carry):
        block = owned_block(step)
        block_copy(block, block).wait_recv()
        skin_ref[block] = skin_of(block)
        answer_copy(block, tile).start()
        return carry

    def rise():
        @pl.when(has_after)
        def _():
            edge_up.wait_send()
            edge_down.wait_recv()

        @pl.when(has_before)
        def _():
            edge_down.wait_send()
            edge_up.wait_recv()

        @pl.when(tile == 0)
        def _():
            halo_ref[0] = jnp.zeros((levels, fields, lanes), jnp.float32)

        @pl.when(tile == tiles - 1)
        def _():
            halo_ref[1] = jnp.zeros((levels, fields, lanes), jnp.float32)

        row = lax.broadcasted_iota(jnp.int32, (fields, rows, lanes), 1)
        first_row = row == 0
        last_row = row == rows - 1
        which = lax.broadcasted_iota(jnp.int32, (fields, rows, lanes), 0)
        mix = jnp.zeros((fields, rows, lanes), jnp.float32)
        for f in range(fields):
            mix = jnp.where(which == f, mixing_ref[f], mix)

        def spread(k):
            field = tracers_ref[k]
            north = jnp.where(first_row, halo_ref[0, k][:, None, :], pltpu.roll(field, 1, 1))
            south = jnp.where(last_row, halo_ref[1, k][:, None, :], pltpu.roll(field, rows - 1, 1))
            along = pltpu.roll(field, 1, 2) + pltpu.roll(field, lanes - 1, 2)
            return mix * (north + south + along - 4.0 * field)

        base_ref[last] = bottom + spread(last)

        def up(step, carry):
            base, slope = carry
            k = levels - 2 - step
            factor = factor_ref[k]
            base = base_ref[k] + factor * base
            slope = factor * slope
            slope_ref[k] = slope
            base_ref[k] = base + spread(k)
            return base, slope

        lax.fori_loop(0, levels - 1, up, (bottom, admittance))

    @pl.when(early)
    def _():
        rise()

    lax.fori_loop(0, side // 2, answer, 0)

    @pl.when(jnp.logical_not(early))
    def _():
        rise()


    total_ref[...] = jnp.zeros_like(total_ref)
    slot_of = lax.broadcasted_iota(jnp.int32, (1, capacity), 1)
    group_of = as_bf16(lax.broadcasted_iota(jnp.int32, (groups, capacity), 0))

    def scatter(blocks, skins):
        hots, lefts = [], []
        for block, skin in zip(blocks, skins):
            hot, group = cells_of(block)
            here = group_of == as_bf16(group)
            area = jnp.where(slot_of < counts_ref[block], areas_ref[pl.ds(block, 1), :], 0.0)
            weight = skin * jnp.where(upper, area[:, :dense], area[:, dense:])
            pieces = []
            for part, area_part in zip(split_two(weight), split_two(area)):
                found = [
                    jnp.concatenate([part[f : f + 1], part[fields + f : fields + f + 1]], axis=1)
                    for f in range(fields)
                ]
                for value in found + [area_part]:
                    spread_value = jnp.broadcast_to(value, (groups, capacity)).astype(jnp.bfloat16)
                    pieces.append(jnp.where(here, spread_value, jnp.zeros((), jnp.bfloat16)))
            hots.append(hot)
            lefts.append(jnp.concatenate(pieces, axis=0))
        total_ref[...] += lax.dot_general(
            jnp.concatenate(hots, axis=1), jnp.concatenate(lefts, axis=1), (((1,), (1,)), ((), ())),
            preferred_element_type=jnp.float32,
        )

    def scatter_owned(blocks):
        scatter(blocks, [skin_ref[block] for block in blocks])

    def scatter_near(blocks):
        for block in blocks:
            block_copy(block, block).wait_recv()
        scatter(blocks, [skin_of(block) for block in blocks])

    def scatter_asked(blocks):
        for block in blocks:
            answer_copy(block, block).wait_recv()
        scatter(blocks, [answer_ref[block] for block in blocks])

    each(side // 2, far_batch, owned_block, scatter_owned)
    each(side, near_batch, near_block, scatter_near)
    each(side // 2, 2, asked_block, scatter_asked)

    sums = (fields + 1) * groups
    totals = total_ref[...].T
    totals = totals[:sums] + totals[sums:]
    for k in range(fields + 1):
        for half in range(halves):
            planes_ref[k, half * groups : (half + 1) * groups, :] = totals[
                k * groups : (k + 1) * groups, half * lanes : (half + 1) * lanes
            ]
    flux_ref[...] = conductance * (planes_ref[0:fields] - bottom * planes_ref[fields : fields + 1])

    def drain(step, carry):
        block_copy(asked_block(step), tile).wait_send()
        answer_copy(owned_block(step), tile).wait_send()
        return carry

    def drain_near(step, carry):
        block_copy(near_block(step), tile).wait_send()
        return carry

    lax.fori_loop(0, side // 2, drain, 0)
    lax.fori_loop(0, side, drain_near, 0)


def finish(base_ref, slope_ref, flux_ref, solved_hbm, surface_hbm, solved_ref, store_sem):
    chunk = base_ref.shape[0] // CHUNKS
    flux_store = pltpu.make_async_copy(flux_ref, surface_hbm, store_sem.at[CHUNKS])
    flux_store.start()
    flux = flux_ref[...]
    stores = []
    for c in range(CHUNKS):
        span = pl.ds(c * chunk, chunk)

        def combine(k, carry):
            solved_ref[k] = base_ref[k] + slope_ref[k] * flux
            return carry

        lax.fori_loop(c * chunk, (c + 1) * chunk, combine, 0, unroll=True)
        stores.append(pltpu.make_async_copy(solved_ref.at[span], solved_hbm.at[span], store_sem.at[c]))
        stores[-1].start()
    flux_store.wait()
    for store in stores:
        store.wait()


def on_device(
    tracers, diffusion, coupling, source, sea_mask, mixing, cell_counts, cell_columns, cell_areas
):
    levels, fields, rows, lanes = tracers.shape[1:]
    tiles, capacity = cell_columns.shape[2:]
    width = 2 * fields
    groups = rows * lanes // WIDE
    f32 = jnp.float32
    grid = jax.ShapeDtypeStruct((levels, fields, rows, lanes), f32)
    vmem = pl.BlockSpec(memory_space=pltpu.VMEM)
    held = [
        pltpu.with_memory_space_constraint(array, pltpu.HBM)
        for array in (
            tracers[0], diffusion[0], coupling[0], source[0], sea_mask[0], cell_columns[0, 0], cell_areas[0, 0]
        )
    ]
    base, slope, flux = pl.pallas_call(
        functools.partial(kernel, tiles),
        out_shape=(grid, grid, jax.ShapeDtypeStruct((fields, rows, lanes), f32)),
        in_specs=[pl.BlockSpec(memory_space=pltpu.HBM)] * 9,
        out_specs=(vmem, vmem, vmem),
        scratch_shapes=[
            pltpu.VMEM((levels, fields, rows, lanes), f32),
            pltpu.VMEM((levels, fields, rows, lanes), f32),
            pltpu.VMEM((fields, rows, lanes), f32),
            pltpu.VMEM((fields, rows, lanes), f32),
            pltpu.VMEM((rows, lanes), jnp.int32),
            pltpu.VMEM((tiles, capacity), jnp.int32),
            pltpu.VMEM((tiles, capacity), f32),
            pltpu.SMEM((fields,), f32),
            pltpu.SMEM((tiles,), jnp.int32),
            pltpu.SemaphoreType.DMA((2 * CHUNKS + 7,)),
            pltpu.VMEM((levels, fields, rows, lanes), f32),
            pltpu.VMEM((fields + 1, rows, lanes), f32),
            pltpu.VMEM((WIDE // lanes, groups * width, lanes), f32),
            pltpu.VMEM((groups * 2 * width, WIDE), jnp.bfloat16),
            pltpu.VMEM((tiles, width, capacity), f32),
            pltpu.VMEM((tiles, width, capacity), f32),
            pltpu.VMEM((tiles, width, capacity // 2), f32),
            pltpu.VMEM((tiles, width, capacity // 2), f32),
            pltpu.VMEM((WIDE, 2 * (fields + 1) * groups), f32),
            pltpu.VMEM((2, levels, fields, lanes), f32),
            pltpu.VMEM((2, levels, fields, lanes), f32),
            pltpu.SemaphoreType.DMA((tiles,)),
            pltpu.SemaphoreType.DMA((tiles,)),
            pltpu.SemaphoreType.DMA((2,)),
            pltpu.SemaphoreType.DMA((2,)),
            pltpu.SemaphoreType.REGULAR,
        ],
        compiler_params=pltpu.CompilerParams(
            collective_id=0, has_side_effects=True, vmem_limit_bytes=48 << 20
        ),
    )(
        pltpu.with_memory_space_constraint(mixing[0], pltpu.HBM),
        pltpu.with_memory_space_constraint(cell_counts[0, 0], pltpu.HBM), *held,
    )
    hbm = pl.BlockSpec(memory_space=pltpu.HBM)
    solved, surface = pl.pallas_call(
        finish,
        out_shape=(grid, jax.ShapeDtypeStruct((fields, rows, lanes), f32)),
        in_specs=[vmem, vmem, vmem],
        out_specs=(hbm, hbm),
        scratch_shapes=[
            pltpu.VMEM((levels, fields, rows, lanes), f32),
            pltpu.SemaphoreType.DMA((CHUNKS + 1,)),
        ],
        compiler_params=pltpu.CompilerParams(vmem_limit_bytes=8 << 20),
    )(base, slope, flux)
    return (solved[None], surface[None])


def solution(mesh):
    in_specs = (
        P("comp", None, None, "tile", None),
        P("comp", None, None, "tile", None),
        P("comp", None, "tile", None),
        P("comp", None, "tile", None),
        P("comp", "tile", None),
        P("comp", None),
        P("comp", "tile", None),
        P("comp", "tile", None, None),
        P("comp", "tile", None, None),
    )
    out_specs = (P("comp", None, None, "tile", None), P("comp", None, "tile", None))
    return jax.shard_map(
        on_device, mesh=mesh, in_specs=in_specs, out_specs=out_specs, check_vma=False
    )
```

```python
import functools

import jax
import jax.numpy as jnp
from jax import lax
from jax.experimental import pallas as pl
from jax.experimental.pallas import tpu as pltpu
from jax.sharding import PartitionSpec as P

MESH = pl.DeviceIdType.MESH
CHUNKS = 4
WIDE = 256
BATCH = 4


def split_two(values):
    high = values.astype(jnp.bfloat16).astype(jnp.float32)
    return high, values - high


def as_bf16(integers):
    return integers.astype(jnp.float32).astype(jnp.bfloat16)


def hot_of(cells, lanes, groups):
    row = cells // lanes
    group = row % groups
    inside = (row // groups) * lanes + cells % lanes
    place = as_bf16(lax.broadcasted_iota(jnp.int32, (WIDE, cells.shape[1]), 0))
    one, zero = jnp.ones((), jnp.bfloat16), jnp.zeros((), jnp.bfloat16)
    return jnp.where(place == as_bf16(inside), one, zero), group


def kernel(
    tiles,
    mixing_hbm, counts_hbm, tracers_hbm, diffusion_hbm, coupling_hbm, source_hbm, mask_hbm, cells_hbm, areas_hbm,
    base_ref, slope_ref, flux_ref,
    tracers_ref, diffusion_ref, coupling_ref, source_ref, mask_ref, cells_ref, areas_ref, mixing_ref, counts_ref,
    load_sem,
    factor_ref, planes_ref, table_ref, table16_ref, own_ref, partner_ref, skin_ref, answer_ref, total_ref,
    edge_ref, halo_ref,
    send_sem, recv_sem, edge_send, edge_recv, word_sem,
):
    levels, fields, rows, lanes = tracers_ref.shape
    capacity = cells_ref.shape[1]
    halves = WIDE // lanes
    groups = rows * lanes // WIDE
    width = 2 * fields
    dense = capacity // 2
    comp = lax.axis_index("comp")
    tile = lax.axis_index("tile")
    other = 1 - comp
    after = lax.rem(tile + 1, tiles)
    before = lax.rem(tile + tiles - 1, tiles)

    side = tiles // 2
    place_in_side = tile % side
    near_base = (tile // side) * side
    far_base = side - near_base

    def near_block(j):
        return near_base + (place_in_side + j) % (side // 2) + (j // (side // 2)) * (side // 2)

    def in_order(first, i):
        part = side // 4
        return (place_in_side + 2 * part - first - 2 * (i % part)) % (2 * part) + (i // part) * 2 * part

    def asked_block(i):
        return far_base + in_order(comp, i)

    def owned_block(i):
        return far_base + in_order(1 - comp, i)

    chunk = levels // CHUNKS

    def level_load(source, target, part, slot):
        span = pl.ds(part * chunk, chunk)
        return pltpu.make_async_copy(source.at[span], target.at[span], load_sem.at[slot])

    tracer_loads = [level_load(tracers_hbm, tracers_ref, c, c) for c in range(CHUNKS)]
    diffusion_loads = [level_load(diffusion_hbm, diffusion_ref, c, CHUNKS + c) for c in range(CHUNKS)]
    pairs = (
        (coupling_hbm, coupling_ref), (source_hbm, source_ref), (mask_hbm, mask_ref),
        (cells_hbm, cells_ref), (areas_hbm, areas_ref), (mixing_hbm, mixing_ref), (counts_hbm, counts_ref),
    )
    rest_loads = [
        pltpu.make_async_copy(held, target, load_sem.at[2 * CHUNKS + i]) for i, (held, target) in enumerate(pairs)
    ]
    for c in range(CHUNKS):
        diffusion_loads[c].start()
        if c >= 1:
            tracer_loads[c - 1].start()
    tracer_loads[CHUNKS - 1].start()
    for load in rest_loads:
        load.start()

    barrier = pltpu.get_barrier_semaphore()

    most = tiles - tiles // 4
    late = tile >= most
    prompt = tile < most
    has_before, has_after = tile > 0, tile < tiles - 1
    is_seam_low, is_seam_high = tile == most - 1, tile == most

    def greet(device_comp, block):
        pl.semaphore_signal(barrier, inc=1, device_id=(device_comp, block), device_id_type=MESH)

    def greet_all(device_comp, first, end):
        def step(block, carry):
            greet(device_comp, block)
            return carry

        lax.fori_loop(first, end, step, 0)

    @pl.when(prompt)
    def _():
        @pl.when(comp == 1)
        def _():
            greet_all(1, 0, tile)
            greet_all(1, tile + 1, most)

        @pl.when(comp == 0)
        def _():
            greet_all(1, 0, most)

        greet_all(other, most, tiles)

    @pl.when(late)
    def _():
        greet_all(0, 0, most)
        greet_all(other, most, tiles)

    @pl.when(jnp.logical_and(late, jnp.logical_not(is_seam_high)))
    def _():
        greet(comp, before)

    @pl.when(jnp.logical_and(tile >= most - 1, has_after))
    def _():
        greet(comp, after)

    def down(k, carry):
        factor, reduced = carry
        here = diffusion_ref[k]
        below = diffusion_ref[k + 1]
        field = tracers_ref[k]
        inverse = 1.0 / (1.0 + here + below - here * factor)
        factor = below * inverse
        reduced = (field + here * reduced) * inverse
        factor_ref[k] = factor
        base_ref[k] = reduced
        edge_ref[0, k] = field[:, rows - 1, :]
        edge_ref[1, k] = field[:, 0, :]
        return factor, reduced

    zeros = jnp.zeros((fields, rows, lanes), jnp.float32)
    factor, reduced = zeros, zeros
    diffusion_loads[0].wait()
    for c in range(CHUNKS):
        if c + 1 < CHUNKS:
            diffusion_loads[c + 1].wait()
        tracer_loads[c].wait()
        end = min((c + 1) * chunk, levels - 1)
        factor, reduced = lax.fori_loop(c * chunk, end, down, (factor, reduced))
    for load in rest_loads:
        load.wait()
    last = levels - 1
    here = diffusion_ref[last]
    field = tracers_ref[last]
    admittance = 1.0 / (1.0 + here - here * factor)
    bottom = (field + here * reduced) * admittance
    edge_ref[0, last] = field[:, rows - 1, :]
    edge_ref[1, last] = field[:, 0, :]
    base_ref[last] = bottom
    slope_ref[last] = admittance
    mask = mask_ref[...].astype(jnp.float32)[None]
    coupling = coupling_ref[...]
    conductance = mask * coupling / (1.0 + coupling * admittance)
    offered = mask * (source_ref[...] + conductance * bottom)
    for k in range(width):
        plane = offered[k] if k < fields else conductance[k - fields]
        for half in range(halves):
            table_ref[half, pl.ds(k, groups, stride=width), :] = plane[half * groups : (half + 1) * groups]
    table = jnp.concatenate([table_ref[half] for half in range(halves)], axis=1)
    high, low = split_two(table.reshape(groups, width, WIDE))
    table16_ref[...] = (
        jnp.concatenate([high, low], axis=1).reshape(groups * 2 * width, WIDE).astype(jnp.bfloat16)
    )

    edge_up = pltpu.make_async_remote_copy(
        src_ref=edge_ref.at[0], dst_ref=halo_ref.at[0], send_sem=edge_send.at[0], recv_sem=edge_recv.at[0],
        device_id=(comp, after), device_id_type=MESH,
    )
    edge_down = pltpu.make_async_remote_copy(
        src_ref=edge_ref.at[1], dst_ref=halo_ref.at[1], send_sem=edge_send.at[1], recv_sem=edge_recv.at[1],
        device_id=(comp, before), device_id_type=MESH,
    )
    def block_copy(block, slot):
        return pltpu.make_async_remote_copy(
            src_ref=own_ref.at[block], dst_ref=partner_ref.at[slot],
            send_sem=send_sem.at[block], recv_sem=recv_sem.at[slot],
            device_id=(other, block), device_id_type=MESH,
        )

    def answer_copy(block, slot):
        return pltpu.make_async_remote_copy(
            src_ref=skin_ref.at[block], dst_ref=answer_ref.at[slot],
            send_sem=send_sem.at[block], recv_sem=recv_sem.at[slot],
            device_id=(other, block), device_id_type=MESH,
        )

    def cells_of(block):
        return hot_of(cells_ref[pl.ds(block, 1), :], lanes, groups)

    def pick(blocks):
        hots, group = zip(*[cells_of(block) for block in blocks])
        found = jnp.dot(table16_ref[...], jnp.concatenate(hots, axis=1), preferred_element_type=jnp.float32)
        size = 2 * width
        chosen = [
            found[g * size : g * size + width] + found[g * size + width : (g + 1) * size] for g in range(groups)
        ]
        group = jnp.broadcast_to(jnp.concatenate(group, axis=1), (width, len(blocks) * capacity))
        stride = 1
        while len(chosen) > 1:
            odd = (group // stride) % 2 == 1
            chosen = [jnp.where(odd, chosen[i + 1], chosen[i]) for i in range(0, len(chosen), 2)]
            stride *= 2
        for i, block in enumerate(blocks):
            own_ref[block] = chosen[0][:, i * capacity : (i + 1) * capacity]

    def each(count, batch, block_of, do, first=0):
        def step(s, carry):
            do([block_of(first + s * batch + i) for i in range(batch)])
            return carry

        if count == batch:
            step(0, 0)
        else:
            lax.fori_loop(0, count // batch, step, 0)

    def pick_and_send(blocks):
        pick(blocks)
        for block in blocks:
            block_copy(block, tile).start()

    far_batch = min(BATCH, side // 2)
    near_batch = min(BATCH, side)
    near_half = min(BATCH, side // 2)
    part = side // 4
    ask_batch = min(BATCH, part)
    early = tile < side

    each(part, ask_batch, asked_block, pick)

    @pl.when(early)
    def _():
        each(part, ask_batch, asked_block, pick, first=part)

    def one_unless_zero(number):
        return (number + tiles - 1) // tiles

    @pl.when(jnp.logical_and(prompt, comp == 1))
    def _():
        pl.semaphore_wait(barrier, 2 * most - 1)
        pl.semaphore_signal(word_sem, inc=1, device_id=(other, tile), device_id_type=MESH)

    @pl.when(jnp.logical_and(prompt, comp == 0))
    def _():
        pl.semaphore_wait(word_sem, 1)

    @pl.when(late)
    def _():
        pl.semaphore_wait(barrier, tiles + 1 + one_unless_zero(tiles - 1 - tile))

    @pl.when(jnp.logical_and(has_after, jnp.logical_not(is_seam_low)))
    def _():
        edge_up.start()

    @pl.when(has_before)
    def _():
        edge_down.start()

    def send(step, carry):
        block_copy(asked_block(step), tile).start()
        return carry

    lax.fori_loop(0, part, send, 0)

    @pl.when(jnp.logical_not(early))
    def _():
        each(part, ask_batch, asked_block, pick, first=part)
        lax.fori_loop(part, 2 * part, send, 0)

    @pl.when(jnp.logical_not(early))
    def _():
        each(side // 2, far_batch, owned_block, pick)

    each(side // 2, near_half, near_block, pick_and_send)

    @pl.when(jnp.logical_and(prompt, comp == 0))
    def _():
        pl.semaphore_wait(barrier, 2 * (tiles - most))
        pl.semaphore_signal(word_sem, inc=1, device_id=(other, tile), device_id_type=MESH)

    @pl.when(jnp.logical_and(prompt, comp == 1))
    def _():
        pl.semaphore_wait(word_sem, 1)

    @pl.when(is_seam_low)
    def _():
        edge_up.start()

    @pl.when(early)
    def _():
        lax.fori_loop(part, 2 * part, send, 0)

    @pl.when(early)
    def _():
        each(side // 2, far_batch, owned_block, pick)
    each(side // 2, near_half, near_block, pick_and_send, first=side // 2)

    upper = lax.broadcasted_iota(jnp.int32, (width, dense), 0) < fields

    def skin_of(block):
        both = own_ref[block] + partner_ref[block]
        turned = pltpu.roll(both, fields, 0)
        offers = jnp.where(upper, both[:, :dense], turned[:, dense:])
        conducts = jnp.where(upper, turned[:, :dense], both[:, dense:])
        return offers / (conducts + 1.0)

    def answer(step, carry):
        block = owned_block(step)
        block_copy(block, block).wait_recv()
        skin_ref[block] = skin_of(block)
        answer_copy(block, tile).start()
        return carry

    def rise():
        @pl.when(has_after)
        def _():
            edge_up.wait_send()
            edge_down.wait_recv()

        @pl.when(has_before)
        def _():
            edge_down.wait_send()
            edge_up.wait_recv()

        @pl.when(tile == 0)
        def _():
            halo_ref[0] = jnp.zeros((levels, fields, lanes), jnp.float32)

        @pl.when(tile == tiles - 1)
        def _():
            halo_ref[1] = jnp.zeros((levels, fields, lanes), jnp.float32)

        row = lax.broadcasted_iota(jnp.int32, (fields, rows, lanes), 1)
        first_row = row == 0
        last_row = row == rows - 1
        which = lax.broadcasted_iota(jnp.int32, (fields, rows, lanes), 0)
        mix = jnp.zeros((fields, rows, lanes), jnp.float32)
        for f in range(fields):
            mix = jnp.where(which == f, mixing_ref[f], mix)

        def spread(k):
            field = tracers_ref[k]
            north = jnp.where(first_row, halo_ref[0, k][:, None, :], pltpu.roll(field, 1, 1))
            south = jnp.where(last_row, halo_ref[1, k][:, None, :], pltpu.roll(field, rows - 1, 1))
            along = pltpu.roll(field, 1, 2) + pltpu.roll(field, lanes - 1, 2)
            return mix * (north + south + along - 4.0 * field)

        base_ref[last] = bottom + spread(last)

        def up(step, carry):
            base, slope = carry
            k = levels - 2 - step
            factor = factor_ref[k]
            base = base_ref[k] + factor * base
            slope = factor * slope
            slope_ref[k] = slope
            base_ref[k] = base + spread(k)
            return base, slope

        lax.fori_loop(0, levels - 1, up, (bottom, admittance))

    @pl.when(early)
    def _():
        rise()

    lax.fori_loop(0, part, answer, 0)

    @pl.when(jnp.logical_not(early))
    def _():
        rise()

    lax.fori_loop(part, 2 * part, answer, 0)


    total_ref[...] = jnp.zeros_like(total_ref)
    slot_of = lax.broadcasted_iota(jnp.int32, (1, capacity), 1)
    group_of = as_bf16(lax.broadcasted_iota(jnp.int32, (groups, capacity), 0))

    def scatter(blocks, skins):
        hots, lefts = [], []
        for block, skin in zip(blocks, skins):
            hot, group = cells_of(block)
            here = group_of == as_bf16(group)
            area = jnp.where(slot_of < counts_ref[block], areas_ref[pl.ds(block, 1), :], 0.0)
            weight = skin * jnp.where(upper, area[:, :dense], area[:, dense:])
            pieces = []
            for part, area_part in zip(split_two(weight), split_two(area)):
                found = [
                    jnp.concatenate([part[f : f + 1], part[fields + f : fields + f + 1]], axis=1)
                    for f in range(fields)
                ]
                for value in found + [area_part]:
                    spread_value = jnp.broadcast_to(value, (groups, capacity)).astype(jnp.bfloat16)
                    pieces.append(jnp.where(here, spread_value, jnp.zeros((), jnp.bfloat16)))
            hots.append(hot)
            lefts.append(jnp.concatenate(pieces, axis=0))
        total_ref[...] += lax.dot_general(
            jnp.concatenate(hots, axis=1), jnp.concatenate(lefts, axis=1), (((1,), (1,)), ((), ())),
            preferred_element_type=jnp.float32,
        )

    def scatter_owned(blocks):
        scatter(blocks, [skin_ref[block] for block in blocks])

    def scatter_near(blocks):
        for block in blocks:
            block_copy(block, block).wait_recv()
        scatter(blocks, [skin_of(block) for block in blocks])

    def scatter_asked(blocks):
        for block in blocks:
            answer_copy(block, block).wait_recv()
        scatter(blocks, [answer_ref[block] for block in blocks])

    each(side // 2, far_batch, owned_block, scatter_owned)
    each(side, near_batch, near_block, scatter_near)
    each(side // 2, 2, asked_block, scatter_asked)

    sums = (fields + 1) * groups
    totals = total_ref[...].T
    totals = totals[:sums] + totals[sums:]
    for k in range(fields + 1):
        for half in range(halves):
            planes_ref[k, half * groups : (half + 1) * groups, :] = totals[
                k * groups : (k + 1) * groups, half * lanes : (half + 1) * lanes
            ]
    flux_ref[...] = conductance * (planes_ref[0:fields] - bottom * planes_ref[fields : fields + 1])

    def drain(step, carry):
        block_copy(asked_block(step), tile).wait_send()
        answer_copy(owned_block(step), tile).wait_send()
        return carry

    def drain_near(step, carry):
        block_copy(near_block(step), tile).wait_send()
        return carry

    lax.fori_loop(0, side // 2, drain, 0)
    lax.fori_loop(0, side, drain_near, 0)


def finish(base_ref, slope_ref, flux_ref, solved_hbm, surface_hbm, solved_ref, store_sem):
    chunk = base_ref.shape[0] // CHUNKS
    flux_store = pltpu.make_async_copy(flux_ref, surface_hbm, store_sem.at[CHUNKS])
    flux_store.start()
    flux = flux_ref[...]
    stores = []
    for c in range(CHUNKS):
        span = pl.ds(c * chunk, chunk)

        def combine(k, carry):
            solved_ref[k] = base_ref[k] + slope_ref[k] * flux
            return carry

        lax.fori_loop(c * chunk, (c + 1) * chunk, combine, 0, unroll=True)
        stores.append(pltpu.make_async_copy(solved_ref.at[span], solved_hbm.at[span], store_sem.at[c]))
        stores[-1].start()
    flux_store.wait()
    for store in stores:
        store.wait()


def on_device(
    tracers, diffusion, coupling, source, sea_mask, mixing, cell_counts, cell_columns, cell_areas
):
    levels, fields, rows, lanes = tracers.shape[1:]
    tiles, capacity = cell_columns.shape[2:]
    width = 2 * fields
    groups = rows * lanes // WIDE
    f32 = jnp.float32
    grid = jax.ShapeDtypeStruct((levels, fields, rows, lanes), f32)
    vmem = pl.BlockSpec(memory_space=pltpu.VMEM)
    held = [
        pltpu.with_memory_space_constraint(array, pltpu.HBM)
        for array in (
            tracers[0], diffusion[0], coupling[0], source[0], sea_mask[0], cell_columns[0, 0], cell_areas[0, 0]
        )
    ]
    base, slope, flux = pl.pallas_call(
        functools.partial(kernel, tiles),
        out_shape=(grid, grid, jax.ShapeDtypeStruct((fields, rows, lanes), f32)),
        in_specs=[pl.BlockSpec(memory_space=pltpu.HBM)] * 9,
        out_specs=(vmem, vmem, vmem),
        scratch_shapes=[
            pltpu.VMEM((levels, fields, rows, lanes), f32),
            pltpu.VMEM((levels, fields, rows, lanes), f32),
            pltpu.VMEM((fields, rows, lanes), f32),
            pltpu.VMEM((fields, rows, lanes), f32),
            pltpu.VMEM((rows, lanes), jnp.int32),
            pltpu.VMEM((tiles, capacity), jnp.int32),
            pltpu.VMEM((tiles, capacity), f32),
            pltpu.SMEM((fields,), f32),
            pltpu.SMEM((tiles,), jnp.int32),
            pltpu.SemaphoreType.DMA((2 * CHUNKS + 7,)),
            pltpu.VMEM((levels, fields, rows, lanes), f32),
            pltpu.VMEM((fields + 1, rows, lanes), f32),
            pltpu.VMEM((WIDE // lanes, groups * width, lanes), f32),
            pltpu.VMEM((groups * 2 * width, WIDE), jnp.bfloat16),
            pltpu.VMEM((tiles, width, capacity), f32),
            pltpu.VMEM((tiles, width, capacity), f32),
            pltpu.VMEM((tiles, width, capacity // 2), f32),
            pltpu.VMEM((tiles, width, capacity // 2), f32),
            pltpu.VMEM((WIDE, 2 * (fields + 1) * groups), f32),
            pltpu.VMEM((2, levels, fields, lanes), f32),
            pltpu.VMEM((2, levels, fields, lanes), f32),
            pltpu.SemaphoreType.DMA((tiles,)),
            pltpu.SemaphoreType.DMA((tiles,)),
            pltpu.SemaphoreType.DMA((2,)),
            pltpu.SemaphoreType.DMA((2,)),
            pltpu.SemaphoreType.REGULAR,
        ],
        compiler_params=pltpu.CompilerParams(
            collective_id=0, has_side_effects=True, vmem_limit_bytes=48 << 20
        ),
    )(
        pltpu.with_memory_space_constraint(mixing[0], pltpu.HBM),
        pltpu.with_memory_space_constraint(cell_counts[0, 0], pltpu.HBM), *held,
    )
    hbm = pl.BlockSpec(memory_space=pltpu.HBM)
    solved, surface = pl.pallas_call(
        finish,
        out_shape=(grid, jax.ShapeDtypeStruct((fields, rows, lanes), f32)),
        in_specs=[vmem, vmem, vmem],
        out_specs=(hbm, hbm),
        scratch_shapes=[
            pltpu.VMEM((levels, fields, rows, lanes), f32),
            pltpu.SemaphoreType.DMA((CHUNKS + 1,)),
        ],
        compiler_params=pltpu.CompilerParams(vmem_limit_bytes=8 << 20),
    )(base, slope, flux)
    return (solved[None], surface[None])


def solution(mesh):
    in_specs = (
        P("comp", None, None, "tile", None),
        P("comp", None, None, "tile", None),
        P("comp", None, "tile", None),
        P("comp", None, "tile", None),
        P("comp", "tile", None),
        P("comp", None),
        P("comp", "tile", None),
        P("comp", "tile", None, None),
        P("comp", "tile", None, None),
    )
    out_specs = (P("comp", None, None, "tile", None), P("comp", None, "tile", None))
    return jax.shard_map(
        on_device, mesh=mesh, in_specs=in_specs, out_specs=out_specs, check_vma=False
    )
```

```python
import functools

import jax
import jax.numpy as jnp
from jax import lax
from jax.experimental import pallas as pl
from jax.experimental.pallas import tpu as pltpu
from jax.sharding import PartitionSpec as P

MESH = pl.DeviceIdType.MESH
CHUNKS = 4
WIDE = 256
BATCH = 4


def split_two(values):
    high = values.astype(jnp.bfloat16).astype(jnp.float32)
    return high, values - high


def as_bf16(integers):
    return integers.astype(jnp.float32).astype(jnp.bfloat16)


def hot_of(cells, lanes, groups):
    row = cells // lanes
    group = row % groups
    inside = (row // groups) * lanes + cells % lanes
    place = as_bf16(lax.broadcasted_iota(jnp.int32, (WIDE, cells.shape[1]), 0))
    one, zero = jnp.ones((), jnp.bfloat16), jnp.zeros((), jnp.bfloat16)
    return jnp.where(place == as_bf16(inside), one, zero), group


def kernel(
    tiles,
    mixing_hbm, counts_hbm, tracers_hbm, diffusion_hbm, coupling_hbm, source_hbm, mask_hbm, cells_hbm, areas_hbm,
    base_ref, slope_ref, flux_ref,
    tracers_ref, diffusion_ref, coupling_ref, source_ref, mask_ref, cells_ref, areas_ref, mixing_ref, counts_ref,
    load_sem,
    factor_ref, planes_ref, table_ref, table16_ref, own_ref, partner_ref, skin_ref, answer_ref, total_ref,
    edge_ref, halo_ref,
    send_sem, recv_sem, edge_send, edge_recv, word_sem,
):
    levels, fields, rows, lanes = tracers_ref.shape
    capacity = cells_ref.shape[1]
    halves = WIDE // lanes
    groups = rows * lanes // WIDE
    width = 2 * fields
    dense = capacity // 2
    comp = lax.axis_index("comp")
    tile = lax.axis_index("tile")
    other = 1 - comp
    after = lax.rem(tile + 1, tiles)
    before = lax.rem(tile + tiles - 1, tiles)

    side = tiles // 2
    place_in_side = tile % side
    near_base = (tile // side) * side
    far_base = side - near_base

    def near_block(j):
        return near_base + (place_in_side + j) % (side // 2) + (j // (side // 2)) * (side // 2)

    def in_order(first, i):
        part = side // 4
        return (place_in_side + 2 * part - first - 2 * (i % part)) % (2 * part) + (i // part) * 2 * part

    def asked_block(i):
        return far_base + in_order(comp, i)

    part = side // 4

    def owned_block(i):
        return far_base + (place_in_side + 1 - comp + 2 * (i % part)) % (2 * part) + (i // part) * 2 * part

    chunk = levels // CHUNKS

    def level_load(source, target, part, slot):
        span = pl.ds(part * chunk, chunk)
        return pltpu.make_async_copy(source.at[span], target.at[span], load_sem.at[slot])

    tracer_loads = [level_load(tracers_hbm, tracers_ref, c, c) for c in range(CHUNKS)]
    diffusion_loads = [level_load(diffusion_hbm, diffusion_ref, c, CHUNKS + c) for c in range(CHUNKS)]
    pairs = (
        (coupling_hbm, coupling_ref), (source_hbm, source_ref), (mask_hbm, mask_ref),
        (cells_hbm, cells_ref), (areas_hbm, areas_ref), (mixing_hbm, mixing_ref), (counts_hbm, counts_ref),
    )
    rest_loads = [
        pltpu.make_async_copy(held, target, load_sem.at[2 * CHUNKS + i]) for i, (held, target) in enumerate(pairs)
    ]
    for c in range(CHUNKS):
        diffusion_loads[c].start()
        if c >= 1:
            tracer_loads[c - 1].start()
    tracer_loads[CHUNKS - 1].start()
    for load in rest_loads:
        load.start()

    barrier = pltpu.get_barrier_semaphore()

    most = tiles - tiles // 4
    late = tile >= most
    prompt = tile < most
    has_before, has_after = tile > 0, tile < tiles - 1
    is_seam_low, is_seam_high = tile == most - 1, tile == most

    def greet(device_comp, block):
        pl.semaphore_signal(barrier, inc=1, device_id=(device_comp, block), device_id_type=MESH)

    def greet_all(device_comp, first, end):
        def step(block, carry):
            greet(device_comp, block)
            return carry

        lax.fori_loop(first, end, step, 0)

    @pl.when(prompt)
    def _():
        @pl.when(comp == 1)
        def _():
            greet_all(1, 0, tile)
            greet_all(1, tile + 1, most)

        @pl.when(comp == 0)
        def _():
            greet_all(1, 0, most)

        greet_all(other, most, tiles)

    @pl.when(late)
    def _():
        greet_all(0, 0, most)
        greet_all(other, most, tiles)

    @pl.when(jnp.logical_and(late, jnp.logical_not(is_seam_high)))
    def _():
        greet(comp, before)

    @pl.when(jnp.logical_and(tile >= most - 1, has_after))
    def _():
        greet(comp, after)

    def down(k, carry):
        factor, reduced = carry
        here = diffusion_ref[k]
        below = diffusion_ref[k + 1]
        field = tracers_ref[k]
        inverse = 1.0 / (1.0 + here + below - here * factor)
        factor = below * inverse
        reduced = (field + here * reduced) * inverse
        factor_ref[k] = factor
        base_ref[k] = reduced
        edge_ref[0, k] = field[:, rows - 1, :]
        edge_ref[1, k] = field[:, 0, :]
        return factor, reduced

    zeros = jnp.zeros((fields, rows, lanes), jnp.float32)
    factor, reduced = zeros, zeros
    diffusion_loads[0].wait()
    for c in range(CHUNKS):
        if c + 1 < CHUNKS:
            diffusion_loads[c + 1].wait()
        tracer_loads[c].wait()
        end = min((c + 1) * chunk, levels - 1)
        factor, reduced = lax.fori_loop(c * chunk, end, down, (factor, reduced))
    for load in rest_loads:
        load.wait()
    last = levels - 1
    here = diffusion_ref[last]
    field = tracers_ref[last]
    admittance = 1.0 / (1.0 + here - here * factor)
    bottom = (field + here * reduced) * admittance
    edge_ref[0, last] = field[:, rows - 1, :]
    edge_ref[1, last] = field[:, 0, :]
    base_ref[last] = bottom
    slope_ref[last] = admittance
    mask = mask_ref[...].astype(jnp.float32)[None]
    coupling = coupling_ref[...]
    conductance = mask * coupling / (1.0 + coupling * admittance)
    offered = mask * (source_ref[...] + conductance * bottom)
    for k in range(width):
        plane = offered[k] if k < fields else conductance[k - fields]
        for half in range(halves):
            table_ref[half, pl.ds(k, groups, stride=width), :] = plane[half * groups : (half + 1) * groups]
    table = jnp.concatenate([table_ref[half] for half in range(halves)], axis=1)
    high, low = split_two(table.reshape(groups, width, WIDE))
    table16_ref[...] = (
        jnp.concatenate([high, low], axis=1).reshape(groups * 2 * width, WIDE).astype(jnp.bfloat16)
    )

    edge_up = pltpu.make_async_remote_copy(
        src_ref=edge_ref.at[0], dst_ref=halo_ref.at[0], send_sem=edge_send.at[0], recv_sem=edge_recv.at[0],
        device_id=(comp, after), device_id_type=MESH,
    )
    edge_down = pltpu.make_async_remote_copy(
        src_ref=edge_ref.at[1], dst_ref=halo_ref.at[1], send_sem=edge_send.at[1], recv_sem=edge_recv.at[1],
        device_id=(comp, before), device_id_type=MESH,
    )
    def block_copy(block, slot):
        return pltpu.make_async_remote_copy(
            src_ref=own_ref.at[block], dst_ref=partner_ref.at[slot],
            send_sem=send_sem.at[block], recv_sem=recv_sem.at[slot],
            device_id=(other, block), device_id_type=MESH,
        )

    def answer_copy(block, slot):
        return pltpu.make_async_remote_copy(
            src_ref=skin_ref.at[block], dst_ref=answer_ref.at[slot],
            send_sem=send_sem.at[block], recv_sem=recv_sem.at[slot],
            device_id=(other, block), device_id_type=MESH,
        )

    def cells_of(block):
        return hot_of(cells_ref[pl.ds(block, 1), :], lanes, groups)

    def pick(blocks):
        hots, group = zip(*[cells_of(block) for block in blocks])
        found = jnp.dot(table16_ref[...], jnp.concatenate(hots, axis=1), preferred_element_type=jnp.float32)
        size = 2 * width
        chosen = [
            found[g * size : g * size + width] + found[g * size + width : (g + 1) * size] for g in range(groups)
        ]
        group = jnp.broadcast_to(jnp.concatenate(group, axis=1), (width, len(blocks) * capacity))
        stride = 1
        while len(chosen) > 1:
            odd = (group // stride) % 2 == 1
            chosen = [jnp.where(odd, chosen[i + 1], chosen[i]) for i in range(0, len(chosen), 2)]
            stride *= 2
        for i, block in enumerate(blocks):
            own_ref[block] = chosen[0][:, i * capacity : (i + 1) * capacity]

    def each(count, batch, block_of, do, first=0):
        def step(s, carry):
            do([block_of(first + s * batch + i) for i in range(batch)])
            return carry

        if count == batch:
            step(0, 0)
        else:
            lax.fori_loop(0, count // batch, step, 0)

    def pick_and_send(blocks):
        pick(blocks)
        for block in blocks:
            block_copy(block, tile).start()

    far_batch = min(BATCH, side // 2)
    near_batch = min(BATCH, side)
    near_half = min(BATCH, side // 2)
    part = side // 4
    ask_batch = min(BATCH, part)
    early = tile < side

    each(part, ask_batch, asked_block, pick)

    @pl.when(early)
    def _():
        each(part, ask_batch, asked_block, pick, first=part)

    def one_unless_zero(number):
        return (number + tiles - 1) // tiles

    @pl.when(jnp.logical_and(prompt, comp == 1))
    def _():
        pl.semaphore_wait(barrier, 2 * most - 1)
        pl.semaphore_signal(word_sem, inc=1, device_id=(other, tile), device_id_type=MESH)

    @pl.when(jnp.logical_and(prompt, comp == 0))
    def _():
        pl.semaphore_wait(word_sem, 1)

    @pl.when(late)
    def _():
        pl.semaphore_wait(barrier, tiles + 1 + one_unless_zero(tiles - 1 - tile))

    @pl.when(jnp.logical_and(has_after, jnp.logical_not(is_seam_low)))
    def _():
        edge_up.start()

    @pl.when(has_before)
    def _():
        edge_down.start()

    def send(step, carry):
        block_copy(asked_block(step), tile).start()
        return carry

    lax.fori_loop(0, part, send, 0)

    @pl.when(jnp.logical_not(early))
    def _():
        each(part, ask_batch, asked_block, pick, first=part)
        lax.fori_loop(part, 2 * part, send, 0)

    each(side // 2, near_half, near_block, pick_and_send)

    @pl.when(jnp.logical_not(early))
    def _():
        each(side // 2, far_batch, owned_block, pick)


    @pl.when(jnp.logical_and(prompt, comp == 0))
    def _():
        pl.semaphore_wait(barrier, 2 * (tiles - most))
        pl.semaphore_signal(word_sem, inc=1, device_id=(other, tile), device_id_type=MESH)

    @pl.when(jnp.logical_and(prompt, comp == 1))
    def _():
        pl.semaphore_wait(word_sem, 1)

    @pl.when(is_seam_low)
    def _():
        edge_up.start()

    @pl.when(early)
    def _():
        lax.fori_loop(part, 2 * part, send, 0)

    each(side // 2, near_half, near_block, pick_and_send, first=side // 2)

    @pl.when(early)
    def _():
        each(side // 2, far_batch, owned_block, pick)

    upper = lax.broadcasted_iota(jnp.int32, (width, dense), 0) < fields

    def skin_of(block):
        both = own_ref[block] + partner_ref[block]
        turned = pltpu.roll(both, fields, 0)
        offers = jnp.where(upper, both[:, :dense], turned[:, dense:])
        conducts = jnp.where(upper, turned[:, :dense], both[:, dense:])
        return offers / (conducts + 1.0)

    def answer(step, carry):
        block = owned_block(step)
        block_copy(block, block).wait_recv()
        skin_ref[block] = skin_of(block)
        answer_copy(block, tile).start()
        return carry

    def rise():
        @pl.when(has_after)
        def _():
            edge_up.wait_send()
            edge_down.wait_recv()

        @pl.when(has_before)
        def _():
            edge_down.wait_send()
            edge_up.wait_recv()

        @pl.when(tile == 0)
        def _():
            halo_ref[0] = jnp.zeros((levels, fields, lanes), jnp.float32)

        @pl.when(tile == tiles - 1)
        def _():
            halo_ref[1] = jnp.zeros((levels, fields, lanes), jnp.float32)

        row = lax.broadcasted_iota(jnp.int32, (fields, rows, lanes), 1)
        first_row = row == 0
        last_row = row == rows - 1
        which = lax.broadcasted_iota(jnp.int32, (fields, rows, lanes), 0)
        mix = jnp.zeros((fields, rows, lanes), jnp.float32)
        for f in range(fields):
            mix = jnp.where(which == f, mixing_ref[f], mix)

        def spread(k):
            field = tracers_ref[k]
            north = jnp.where(first_row, halo_ref[0, k][:, None, :], pltpu.roll(field, 1, 1))
            south = jnp.where(last_row, halo_ref[1, k][:, None, :], pltpu.roll(field, rows - 1, 1))
            along = pltpu.roll(field, 1, 2) + pltpu.roll(field, lanes - 1, 2)
            return mix * (north + south + along - 4.0 * field)

        base_ref[last] = bottom + spread(last)

        def up(step, carry):
            base, slope = carry
            k = levels - 2 - step
            factor = factor_ref[k]
            base = base_ref[k] + factor * base
            slope = factor * slope
            slope_ref[k] = slope
            base_ref[k] = base + spread(k)
            return base, slope

        lax.fori_loop(0, levels - 1, up, (bottom, admittance))

    @pl.when(early)
    def _():
        rise()

    lax.fori_loop(0, part, answer, 0)

    @pl.when(jnp.logical_not(early))
    def _():
        rise()

    lax.fori_loop(part, 2 * part, answer, 0)


    total_ref[...] = jnp.zeros_like(total_ref)
    slot_of = lax.broadcasted_iota(jnp.int32, (1, capacity), 1)
    group_of = as_bf16(lax.broadcasted_iota(jnp.int32, (groups, capacity), 0))

    def scatter(blocks, skins):
        hots, lefts = [], []
        for block, skin in zip(blocks, skins):
            hot, group = cells_of(block)
            here = group_of == as_bf16(group)
            area = jnp.where(slot_of < counts_ref[block], areas_ref[pl.ds(block, 1), :], 0.0)
            weight = skin * jnp.where(upper, area[:, :dense], area[:, dense:])
            pieces = []
            for part, area_part in zip(split_two(weight), split_two(area)):
                found = [
                    jnp.concatenate([part[f : f + 1], part[fields + f : fields + f + 1]], axis=1)
                    for f in range(fields)
                ]
                for value in found + [area_part]:
                    spread_value = jnp.broadcast_to(value, (groups, capacity)).astype(jnp.bfloat16)
                    pieces.append(jnp.where(here, spread_value, jnp.zeros((), jnp.bfloat16)))
            hots.append(hot)
            lefts.append(jnp.concatenate(pieces, axis=0))
        total_ref[...] += lax.dot_general(
            jnp.concatenate(hots, axis=1), jnp.concatenate(lefts, axis=1), (((1,), (1,)), ((), ())),
            preferred_element_type=jnp.float32,
        )

    def scatter_owned(blocks):
        scatter(blocks, [skin_ref[block] for block in blocks])

    def scatter_near(blocks):
        for block in blocks:
            block_copy(block, block).wait_recv()
        scatter(blocks, [skin_of(block) for block in blocks])

    def scatter_asked(blocks):
        for block in blocks:
            answer_copy(block, block).wait_recv()
        scatter(blocks, [answer_ref[block] for block in blocks])

    each(side // 2, far_batch, owned_block, scatter_owned)
    each(side, near_batch, near_block, scatter_near)
    each(side // 2, 2, asked_block, scatter_asked)

    sums = (fields + 1) * groups
    totals = total_ref[...].T
    totals = totals[:sums] + totals[sums:]
    for k in range(fields + 1):
        for half in range(halves):
            planes_ref[k, half * groups : (half + 1) * groups, :] = totals[
                k * groups : (k + 1) * groups, half * lanes : (half + 1) * lanes
            ]
    flux_ref[...] = conductance * (planes_ref[0:fields] - bottom * planes_ref[fields : fields + 1])

    def drain(step, carry):
        block_copy(asked_block(step), tile).wait_send()
        answer_copy(owned_block(step), tile).wait_send()
        return carry

    def drain_near(step, carry):
        block_copy(near_block(step), tile).wait_send()
        return carry

    lax.fori_loop(0, side // 2, drain, 0)
    lax.fori_loop(0, side, drain_near, 0)


def finish(base_ref, slope_ref, flux_ref, solved_hbm, surface_hbm, solved_ref, store_sem):
    chunk = base_ref.shape[0] // CHUNKS
    flux_store = pltpu.make_async_copy(flux_ref, surface_hbm, store_sem.at[CHUNKS])
    flux_store.start()
    flux = flux_ref[...]
    stores = []
    for c in range(CHUNKS):
        span = pl.ds(c * chunk, chunk)

        def combine(k, carry):
            solved_ref[k] = base_ref[k] + slope_ref[k] * flux
            return carry

        lax.fori_loop(c * chunk, (c + 1) * chunk, combine, 0, unroll=True)
        stores.append(pltpu.make_async_copy(solved_ref.at[span], solved_hbm.at[span], store_sem.at[c]))
        stores[-1].start()
    flux_store.wait()
    for store in stores:
        store.wait()


def on_device(
    tracers, diffusion, coupling, source, sea_mask, mixing, cell_counts, cell_columns, cell_areas
):
    levels, fields, rows, lanes = tracers.shape[1:]
    tiles, capacity = cell_columns.shape[2:]
    width = 2 * fields
    groups = rows * lanes // WIDE
    f32 = jnp.float32
    grid = jax.ShapeDtypeStruct((levels, fields, rows, lanes), f32)
    vmem = pl.BlockSpec(memory_space=pltpu.VMEM)
    held = [
        pltpu.with_memory_space_constraint(array, pltpu.HBM)
        for array in (
            tracers[0], diffusion[0], coupling[0], source[0], sea_mask[0], cell_columns[0, 0], cell_areas[0, 0]
        )
    ]
    base, slope, flux = pl.pallas_call(
        functools.partial(kernel, tiles),
        out_shape=(grid, grid, jax.ShapeDtypeStruct((fields, rows, lanes), f32)),
        in_specs=[pl.BlockSpec(memory_space=pltpu.HBM)] * 9,
        out_specs=(vmem, vmem, vmem),
        scratch_shapes=[
            pltpu.VMEM((levels, fields, rows, lanes), f32),
            pltpu.VMEM((levels, fields, rows, lanes), f32),
            pltpu.VMEM((fields, rows, lanes), f32),
            pltpu.VMEM((fields, rows, lanes), f32),
            pltpu.VMEM((rows, lanes), jnp.int32),
            pltpu.VMEM((tiles, capacity), jnp.int32),
            pltpu.VMEM((tiles, capacity), f32),
            pltpu.SMEM((fields,), f32),
            pltpu.SMEM((tiles,), jnp.int32),
            pltpu.SemaphoreType.DMA((2 * CHUNKS + 7,)),
            pltpu.VMEM((levels, fields, rows, lanes), f32),
            pltpu.VMEM((fields + 1, rows, lanes), f32),
            pltpu.VMEM((WIDE // lanes, groups * width, lanes), f32),
            pltpu.VMEM((groups * 2 * width, WIDE), jnp.bfloat16),
            pltpu.VMEM((tiles, width, capacity), f32),
            pltpu.VMEM((tiles, width, capacity), f32),
            pltpu.VMEM((tiles, width, capacity // 2), f32),
            pltpu.VMEM((tiles, width, capacity // 2), f32),
            pltpu.VMEM((WIDE, 2 * (fields + 1) * groups), f32),
            pltpu.VMEM((2, levels, fields, lanes), f32),
            pltpu.VMEM((2, levels, fields, lanes), f32),
            pltpu.SemaphoreType.DMA((tiles,)),
            pltpu.SemaphoreType.DMA((tiles,)),
            pltpu.SemaphoreType.DMA((2,)),
            pltpu.SemaphoreType.DMA((2,)),
            pltpu.SemaphoreType.REGULAR,
        ],
        compiler_params=pltpu.CompilerParams(
            collective_id=0, has_side_effects=True, vmem_limit_bytes=48 << 20
        ),
    )(
        pltpu.with_memory_space_constraint(mixing[0], pltpu.HBM),
        pltpu.with_memory_space_constraint(cell_counts[0, 0], pltpu.HBM), *held,
    )
    hbm = pl.BlockSpec(memory_space=pltpu.HBM)
    solved, surface = pl.pallas_call(
        finish,
        out_shape=(grid, jax.ShapeDtypeStruct((fields, rows, lanes), f32)),
        in_specs=[vmem, vmem, vmem],
        out_specs=(hbm, hbm),
        scratch_shapes=[
            pltpu.VMEM((levels, fields, rows, lanes), f32),
            pltpu.SemaphoreType.DMA((CHUNKS + 1,)),
        ],
        compiler_params=pltpu.CompilerParams(vmem_limit_bytes=8 << 20),
    )(base, slope, flux)
    return (solved[None], surface[None])


def solution(mesh):
    in_specs = (
        P("comp", None, None, "tile", None),
        P("comp", None, None, "tile", None),
        P("comp", None, "tile", None),
        P("comp", None, "tile", None),
        P("comp", "tile", None),
        P("comp", None),
        P("comp", "tile", None),
        P("comp", "tile", None, None),
        P("comp", "tile", None, None),
    )
    out_specs = (P("comp", None, None, "tile", None), P("comp", None, "tile", None))
    return jax.shard_map(
        on_device, mesh=mesh, in_specs=in_specs, out_specs=out_specs, check_vma=False
    )
```

```python
import functools

import jax
import jax.numpy as jnp
from jax import lax
from jax.experimental import pallas as pl
from jax.experimental.pallas import tpu as pltpu
from jax.sharding import PartitionSpec as P

MESH = pl.DeviceIdType.MESH
CHUNKS = 2
WIDE = 256
BATCH = 4


def split_two(values):
    high = values.astype(jnp.bfloat16).astype(jnp.float32)
    return high, values - high


def as_bf16(integers):
    return integers.astype(jnp.float32).astype(jnp.bfloat16)


def hot_of(cells, lanes, groups):
    row = cells // lanes
    group = row % groups
    inside = (row // groups) * lanes + cells % lanes
    place = as_bf16(lax.broadcasted_iota(jnp.int32, (WIDE, cells.shape[1]), 0))
    one, zero = jnp.ones((), jnp.bfloat16), jnp.zeros((), jnp.bfloat16)
    return jnp.where(place == as_bf16(inside), one, zero), group


def kernel(
    tiles,
    mixing_hbm, counts_hbm, tracers_hbm, diffusion_hbm, coupling_hbm, source_hbm, mask_hbm, cells_hbm, areas_hbm,
    base_ref, slope_ref, flux_ref,
    tracers_ref, diffusion_ref, coupling_ref, source_ref, mask_ref, cells_ref, areas_ref, mixing_ref, counts_ref,
    load_sem,
    factor_ref, planes_ref, table_ref, table16_ref, own_ref, partner_ref, skin_ref, answer_ref, total_ref,
    edge_ref, halo_ref,
    send_sem, recv_sem, edge_send, edge_recv, word_sem,
):
    levels, fields, rows, lanes = tracers_ref.shape
    capacity = cells_ref.shape[1]
    halves = WIDE // lanes
    groups = rows * lanes // WIDE
    width = 2 * fields
    dense = capacity // 2
    comp = lax.axis_index("comp")
    tile = lax.axis_index("tile")
    other = 1 - comp
    after = lax.rem(tile + 1, tiles)
    before = lax.rem(tile + tiles - 1, tiles)

    side = tiles // 2
    place_in_side = tile % side
    near_base = (tile // side) * side
    far_base = side - near_base

    def near_block(j):
        return near_base + (place_in_side + j) % (side // 2) + (j // (side // 2)) * (side // 2)

    def in_order(first, i):
        part = side // 4
        return (place_in_side + 2 * part - first - 2 * (i % part)) % (2 * part) + (i // part) * 2 * part

    def asked_block(i):
        return far_base + in_order(comp, i)

    part = side // 4

    def owned_block(i):
        return far_base + (place_in_side + 1 - comp + 2 * (i % part)) % (2 * part) + (i // part) * 2 * part

    chunk = levels // CHUNKS

    def level_load(source, target, part, slot):
        span = pl.ds(part * chunk, chunk)
        return pltpu.make_async_copy(source.at[span], target.at[span], load_sem.at[slot])

    tracer_loads = [level_load(tracers_hbm, tracers_ref, c, c) for c in range(CHUNKS)]
    diffusion_loads = [level_load(diffusion_hbm, diffusion_ref, c, CHUNKS + c) for c in range(CHUNKS)]
    pairs = (
        (coupling_hbm, coupling_ref), (source_hbm, source_ref), (mask_hbm, mask_ref),
        (cells_hbm, cells_ref), (areas_hbm, areas_ref), (mixing_hbm, mixing_ref), (counts_hbm, counts_ref),
    )
    rest_loads = [
        pltpu.make_async_copy(held, target, load_sem.at[2 * CHUNKS + i]) for i, (held, target) in enumerate(pairs)
    ]
    for c in range(CHUNKS):
        diffusion_loads[c].start()
        if c >= 1:
            tracer_loads[c - 1].start()
    tracer_loads[CHUNKS - 1].start()
    for load in rest_loads:
        load.start()

    barrier = pltpu.get_barrier_semaphore()

    most = tiles - tiles // 4
    late = tile >= most
    prompt = tile < most
    has_before, has_after = tile > 0, tile < tiles - 1
    is_seam_low, is_seam_high = tile == most - 1, tile == most

    def greet(device_comp, block):
        pl.semaphore_signal(barrier, inc=1, device_id=(device_comp, block), device_id_type=MESH)

    def greet_all(device_comp, first, end):
        def step(block, carry):
            greet(device_comp, block)
            return carry

        lax.fori_loop(first, end, step, 0)

    @pl.when(prompt)
    def _():
        @pl.when(comp == 1)
        def _():
            greet_all(1, 0, tile)
            greet_all(1, tile + 1, most)

        @pl.when(comp == 0)
        def _():
            greet_all(1, 0, most)

        greet_all(other, most, tiles)

    @pl.when(late)
    def _():
        greet_all(0, 0, most)
        greet_all(other, most, tiles)

    @pl.when(jnp.logical_and(late, jnp.logical_not(is_seam_high)))
    def _():
        greet(comp, before)

    @pl.when(jnp.logical_and(tile >= most - 1, has_after))
    def _():
        greet(comp, after)

    def down(k, carry):
        factor, reduced = carry
        here = diffusion_ref[k]
        below = diffusion_ref[k + 1]
        field = tracers_ref[k]
        inverse = 1.0 / (1.0 + here + below - here * factor)
        factor = below * inverse
        reduced = (field + here * reduced) * inverse
        factor_ref[k] = factor
        base_ref[k] = reduced
        edge_ref[0, k] = field[:, rows - 1, :]
        edge_ref[1, k] = field[:, 0, :]
        return factor, reduced

    zeros = jnp.zeros((fields, rows, lanes), jnp.float32)
    factor, reduced = zeros, zeros
    diffusion_loads[0].wait()
    for c in range(CHUNKS):
        if c + 1 < CHUNKS:
            diffusion_loads[c + 1].wait()
        tracer_loads[c].wait()
        end = min((c + 1) * chunk, levels - 1)
        factor, reduced = lax.fori_loop(c * chunk, end, down, (factor, reduced))
    for load in rest_loads:
        load.wait()
    last = levels - 1
    here = diffusion_ref[last]
    field = tracers_ref[last]
    admittance = 1.0 / (1.0 + here - here * factor)
    bottom = (field + here * reduced) * admittance
    edge_ref[0, last] = field[:, rows - 1, :]
    edge_ref[1, last] = field[:, 0, :]
    base_ref[last] = bottom
    slope_ref[last] = admittance
    mask = mask_ref[...].astype(jnp.float32)[None]
    coupling = coupling_ref[...]
    conductance = mask * coupling / (1.0 + coupling * admittance)
    offered = mask * (source_ref[...] + conductance * bottom)
    for k in range(width):
        plane = offered[k] if k < fields else conductance[k - fields]
        for half in range(halves):
            table_ref[half, pl.ds(k, groups, stride=width), :] = plane[half * groups : (half + 1) * groups]
    table = jnp.concatenate([table_ref[half] for half in range(halves)], axis=1)
    high, low = split_two(table.reshape(groups, width, WIDE))
    table16_ref[...] = (
        jnp.concatenate([high, low], axis=1).reshape(groups * 2 * width, WIDE).astype(jnp.bfloat16)
    )

    edge_up = pltpu.make_async_remote_copy(
        src_ref=edge_ref.at[0], dst_ref=halo_ref.at[0], send_sem=edge_send.at[0], recv_sem=edge_recv.at[0],
        device_id=(comp, after), device_id_type=MESH,
    )
    edge_down = pltpu.make_async_remote_copy(
        src_ref=edge_ref.at[1], dst_ref=halo_ref.at[1], send_sem=edge_send.at[1], recv_sem=edge_recv.at[1],
        device_id=(comp, before), device_id_type=MESH,
    )
    def block_copy(block, slot):
        return pltpu.make_async_remote_copy(
            src_ref=own_ref.at[block], dst_ref=partner_ref.at[slot],
            send_sem=send_sem.at[block], recv_sem=recv_sem.at[slot],
            device_id=(other, block), device_id_type=MESH,
        )

    def answer_copy(block, slot):
        return pltpu.make_async_remote_copy(
            src_ref=skin_ref.at[block], dst_ref=answer_ref.at[slot],
            send_sem=send_sem.at[block], recv_sem=recv_sem.at[slot],
            device_id=(other, block), device_id_type=MESH,
        )

    def cells_of(block):
        return hot_of(cells_ref[pl.ds(block, 1), :], lanes, groups)

    def pick(blocks):
        hots, group = zip(*[cells_of(block) for block in blocks])
        found = jnp.dot(table16_ref[...], jnp.concatenate(hots, axis=1), preferred_element_type=jnp.float32)
        size = 2 * width
        chosen = [
            found[g * size : g * size + width] + found[g * size + width : (g + 1) * size] for g in range(groups)
        ]
        group = jnp.broadcast_to(jnp.concatenate(group, axis=1), (width, len(blocks) * capacity))
        stride = 1
        while len(chosen) > 1:
            odd = (group // stride) % 2 == 1
            chosen = [jnp.where(odd, chosen[i + 1], chosen[i]) for i in range(0, len(chosen), 2)]
            stride *= 2
        for i, block in enumerate(blocks):
            own_ref[block] = chosen[0][:, i * capacity : (i + 1) * capacity]

    def each(count, batch, block_of, do, first=0):
        def step(s, carry):
            do([block_of(first + s * batch + i) for i in range(batch)])
            return carry

        if count == batch:
            step(0, 0)
        else:
            lax.fori_loop(0, count // batch, step, 0)

    def pick_and_send(blocks):
        pick(blocks)
        for block in blocks:
            block_copy(block, tile).start()

    far_batch = min(BATCH, side // 2)
    near_batch = min(BATCH, side)
    near_half = min(BATCH, side // 2)
    part = side // 4
    ask_batch = min(BATCH, part)
    early = tile < side

    each(part, ask_batch, asked_block, pick)

    @pl.when(early)
    def _():
        each(part, ask_batch, asked_block, pick, first=part)

    def one_unless_zero(number):
        return (number + tiles - 1) // tiles

    @pl.when(jnp.logical_and(prompt, comp == 1))
    def _():
        pl.semaphore_wait(barrier, 2 * most - 1)
        pl.semaphore_signal(word_sem, inc=1, device_id=(other, tile), device_id_type=MESH)

    @pl.when(jnp.logical_and(prompt, comp == 0))
    def _():
        pl.semaphore_wait(word_sem, 1)

    @pl.when(late)
    def _():
        pl.semaphore_wait(barrier, tiles + 1 + one_unless_zero(tiles - 1 - tile))

    @pl.when(jnp.logical_and(has_after, jnp.logical_not(is_seam_low)))
    def _():
        edge_up.start()

    @pl.when(has_before)
    def _():
        edge_down.start()

    def send(step, carry):
        block_copy(asked_block(step), tile).start()
        return carry

    lax.fori_loop(0, part, send, 0)

    @pl.when(jnp.logical_not(early))
    def _():
        each(part, ask_batch, asked_block, pick, first=part)
        lax.fori_loop(part, 2 * part, send, 0)

    each(side // 2, near_half, near_block, pick_and_send)

    @pl.when(jnp.logical_not(early))
    def _():
        each(side // 2, far_batch, owned_block, pick)


    @pl.when(jnp.logical_and(prompt, comp == 0))
    def _():
        pl.semaphore_wait(barrier, 2 * (tiles - most))
        pl.semaphore_signal(word_sem, inc=1, device_id=(other, tile), device_id_type=MESH)

    @pl.when(jnp.logical_and(prompt, comp == 1))
    def _():
        pl.semaphore_wait(word_sem, 1)

    @pl.when(is_seam_low)
    def _():
        edge_up.start()

    @pl.when(early)
    def _():
        lax.fori_loop(part, 2 * part, send, 0)

    each(side // 2, near_half, near_block, pick_and_send, first=side // 2)

    @pl.when(early)
    def _():
        each(side // 2, far_batch, owned_block, pick)

    upper = lax.broadcasted_iota(jnp.int32, (width, dense), 0) < fields

    def skin_of(block):
        both = own_ref[block] + partner_ref[block]
        turned = pltpu.roll(both, fields, 0)
        offers = jnp.where(upper, both[:, :dense], turned[:, dense:])
        conducts = jnp.where(upper, turned[:, :dense], both[:, dense:])
        return offers / (conducts + 1.0)

    def answer(step, carry):
        block = owned_block(step)
        block_copy(block, block).wait_recv()
        skin_ref[block] = skin_of(block)
        answer_copy(block, tile).start()
        return carry

    def rise():
        @pl.when(has_after)
        def _():
            edge_up.wait_send()
            edge_down.wait_recv()

        @pl.when(has_before)
        def _():
            edge_down.wait_send()
            edge_up.wait_recv()

        @pl.when(tile == 0)
        def _():
            halo_ref[0] = jnp.zeros((levels, fields, lanes), jnp.float32)

        @pl.when(tile == tiles - 1)
        def _():
            halo_ref[1] = jnp.zeros((levels, fields, lanes), jnp.float32)

        row = lax.broadcasted_iota(jnp.int32, (fields, rows, lanes), 1)
        first_row = row == 0
        last_row = row == rows - 1
        which = lax.broadcasted_iota(jnp.int32, (fields, rows, lanes), 0)
        mix = jnp.zeros((fields, rows, lanes), jnp.float32)
        for f in range(fields):
            mix = jnp.where(which == f, mixing_ref[f], mix)

        def spread(k):
            field = tracers_ref[k]
            north = jnp.where(first_row, halo_ref[0, k][:, None, :], pltpu.roll(field, 1, 1))
            south = jnp.where(last_row, halo_ref[1, k][:, None, :], pltpu.roll(field, rows - 1, 1))
            along = pltpu.roll(field, 1, 2) + pltpu.roll(field, lanes - 1, 2)
            return mix * (north + south + along - 4.0 * field)

        base_ref[last] = bottom + spread(last)

        def up(step, carry):
            base, slope = carry
            k = levels - 2 - step
            factor = factor_ref[k]
            base = base_ref[k] + factor * base
            slope = factor * slope
            slope_ref[k] = slope
            base_ref[k] = base + spread(k)
            return base, slope

        lax.fori_loop(0, levels - 1, up, (bottom, admittance))

    at_seam = tile == side - 1
    rise_first = jnp.logical_and(early, jnp.logical_not(at_seam))

    @pl.when(rise_first)
    def _():
        rise()

    lax.fori_loop(0, part, answer, 0)

    @pl.when(jnp.logical_not(rise_first))
    def _():
        rise()

    lax.fori_loop(part, 2 * part, answer, 0)


    total_ref[...] = jnp.zeros_like(total_ref)
    slot_of = lax.broadcasted_iota(jnp.int32, (1, capacity), 1)
    group_of = as_bf16(lax.broadcasted_iota(jnp.int32, (groups, capacity), 0))

    def scatter(blocks, skins):
        hots, lefts = [], []
        for block, skin in zip(blocks, skins):
            hot, group = cells_of(block)
            here = group_of == as_bf16(group)
            area = jnp.where(slot_of < counts_ref[block], areas_ref[pl.ds(block, 1), :], 0.0)
            weight = skin * jnp.where(upper, area[:, :dense], area[:, dense:])
            pieces = []
            for part, area_part in zip(split_two(weight), split_two(area)):
                found = [
                    jnp.concatenate([part[f : f + 1], part[fields + f : fields + f + 1]], axis=1)
                    for f in range(fields)
                ]
                for value in found + [area_part]:
                    spread_value = jnp.broadcast_to(value, (groups, capacity)).astype(jnp.bfloat16)
                    pieces.append(jnp.where(here, spread_value, jnp.zeros((), jnp.bfloat16)))
            hots.append(hot)
            lefts.append(jnp.concatenate(pieces, axis=0))
        total_ref[...] += lax.dot_general(
            jnp.concatenate(hots, axis=1), jnp.concatenate(lefts, axis=1), (((1,), (1,)), ((), ())),
            preferred_element_type=jnp.float32,
        )

    def scatter_owned(blocks):
        scatter(blocks, [skin_ref[block] for block in blocks])

    def scatter_near(blocks):
        for block in blocks:
            block_copy(block, block).wait_recv()
        scatter(blocks, [skin_of(block) for block in blocks])

    def scatter_asked(blocks):
        for block in blocks:
            answer_copy(block, block).wait_recv()
        scatter(blocks, [answer_ref[block] for block in blocks])

    each(side // 2, far_batch, owned_block, scatter_owned)
    each(side, near_batch, near_block, scatter_near)
    each(side // 2, 2, asked_block, scatter_asked)

    sums = (fields + 1) * groups
    totals = total_ref[...].T
    totals = totals[:sums] + totals[sums:]
    for k in range(fields + 1):
        for half in range(halves):
            planes_ref[k, half * groups : (half + 1) * groups, :] = totals[
                k * groups : (k + 1) * groups, half * lanes : (half + 1) * lanes
            ]
    flux_ref[...] = conductance * (planes_ref[0:fields] - bottom * planes_ref[fields : fields + 1])

    def drain(step, carry):
        block_copy(asked_block(step), tile).wait_send()
        answer_copy(owned_block(step), tile).wait_send()
        return carry

    def drain_near(step, carry):
        block_copy(near_block(step), tile).wait_send()
        return carry

    lax.fori_loop(0, side // 2, drain, 0)
    lax.fori_loop(0, side, drain_near, 0)


def finish(base_ref, slope_ref, flux_ref, solved_hbm, surface_hbm, solved_ref, store_sem):
    chunk = base_ref.shape[0] // CHUNKS
    flux_store = pltpu.make_async_copy(flux_ref, surface_hbm, store_sem.at[CHUNKS])
    flux_store.start()
    flux = flux_ref[...]
    stores = []
    for c in range(CHUNKS):
        span = pl.ds(c * chunk, chunk)

        def combine(k, carry):
            solved_ref[k] = base_ref[k] + slope_ref[k] * flux
            return carry

        lax.fori_loop(c * chunk, (c + 1) * chunk, combine, 0, unroll=True)
        stores.append(pltpu.make_async_copy(solved_ref.at[span], solved_hbm.at[span], store_sem.at[c]))
        stores[-1].start()
    flux_store.wait()
    for store in stores:
        store.wait()


def on_device(
    tracers, diffusion, coupling, source, sea_mask, mixing, cell_counts, cell_columns, cell_areas
):
    levels, fields, rows, lanes = tracers.shape[1:]
    tiles, capacity = cell_columns.shape[2:]
    width = 2 * fields
    groups = rows * lanes // WIDE
    f32 = jnp.float32
    grid = jax.ShapeDtypeStruct((levels, fields, rows, lanes), f32)
    vmem = pl.BlockSpec(memory_space=pltpu.VMEM)
    held = [
        pltpu.with_memory_space_constraint(array, pltpu.HBM)
        for array in (
            tracers[0], diffusion[0], coupling[0], source[0], sea_mask[0], cell_columns[0, 0], cell_areas[0, 0]
        )
    ]
    base, slope, flux = pl.pallas_call(
        functools.partial(kernel, tiles),
        out_shape=(grid, grid, jax.ShapeDtypeStruct((fields, rows, lanes), f32)),
        in_specs=[pl.BlockSpec(memory_space=pltpu.HBM)] * 9,
        out_specs=(vmem, vmem, vmem),
        scratch_shapes=[
            pltpu.VMEM((levels, fields, rows, lanes), f32),
            pltpu.VMEM((levels, fields, rows, lanes), f32),
            pltpu.VMEM((fields, rows, lanes), f32),
            pltpu.VMEM((fields, rows, lanes), f32),
            pltpu.VMEM((rows, lanes), jnp.int32),
            pltpu.VMEM((tiles, capacity), jnp.int32),
            pltpu.VMEM((tiles, capacity), f32),
            pltpu.SMEM((fields,), f32),
            pltpu.SMEM((tiles,), jnp.int32),
            pltpu.SemaphoreType.DMA((2 * CHUNKS + 7,)),
            pltpu.VMEM((levels, fields, rows, lanes), f32),
            pltpu.VMEM((fields + 1, rows, lanes), f32),
            pltpu.VMEM((WIDE // lanes, groups * width, lanes), f32),
            pltpu.VMEM((groups * 2 * width, WIDE), jnp.bfloat16),
            pltpu.VMEM((tiles, width, capacity), f32),
            pltpu.VMEM((tiles, width, capacity), f32),
            pltpu.VMEM((tiles, width, capacity // 2), f32),
            pltpu.VMEM((tiles, width, capacity // 2), f32),
            pltpu.VMEM((WIDE, 2 * (fields + 1) * groups), f32),
            pltpu.VMEM((2, levels, fields, lanes), f32),
            pltpu.VMEM((2, levels, fields, lanes), f32),
            pltpu.SemaphoreType.DMA((tiles,)),
            pltpu.SemaphoreType.DMA((tiles,)),
            pltpu.SemaphoreType.DMA((2,)),
            pltpu.SemaphoreType.DMA((2,)),
            pltpu.SemaphoreType.REGULAR,
        ],
        compiler_params=pltpu.CompilerParams(
            collective_id=0, has_side_effects=True, vmem_limit_bytes=48 << 20
        ),
    )(
        pltpu.with_memory_space_constraint(mixing[0], pltpu.HBM),
        pltpu.with_memory_space_constraint(cell_counts[0, 0], pltpu.HBM), *held,
    )
    hbm = pl.BlockSpec(memory_space=pltpu.HBM)
    solved, surface = pl.pallas_call(
        finish,
        out_shape=(grid, jax.ShapeDtypeStruct((fields, rows, lanes), f32)),
        in_specs=[vmem, vmem, vmem],
        out_specs=(hbm, hbm),
        scratch_shapes=[
            pltpu.VMEM((levels, fields, rows, lanes), f32),
            pltpu.SemaphoreType.DMA((CHUNKS + 1,)),
        ],
        compiler_params=pltpu.CompilerParams(vmem_limit_bytes=8 << 20),
    )(base, slope, flux)
    return (solved[None], surface[None])


def solution(mesh):
    in_specs = (
        P("comp", None, None, "tile", None),
        P("comp", None, None, "tile", None),
        P("comp", None, "tile", None),
        P("comp", None, "tile", None),
        P("comp", "tile", None),
        P("comp", None),
        P("comp", "tile", None),
        P("comp", "tile", None, None),
        P("comp", "tile", None, None),
    )
    out_specs = (P("comp", None, None, "tile", None), P("comp", None, "tile", None))
    return jax.shard_map(
        on_device, mesh=mesh, in_specs=in_specs, out_specs=out_specs, check_vma=False
    )
```

```python
import functools

import jax
import jax.numpy as jnp
from jax import lax
from jax.experimental import pallas as pl
from jax.experimental.pallas import tpu as pltpu
from jax.sharding import PartitionSpec as P

MESH = pl.DeviceIdType.MESH
CHUNKS = 4
WIDE = 256
BATCH = 4


def split_two(values):
    high = values.astype(jnp.bfloat16).astype(jnp.float32)
    return high, values - high


def as_bf16(integers):
    return integers.astype(jnp.float32).astype(jnp.bfloat16)


def hot_of(cells, lanes, groups):
    row = cells // lanes
    group = row % groups
    inside = (row // groups) * lanes + cells % lanes
    place = as_bf16(lax.broadcasted_iota(jnp.int32, (WIDE, cells.shape[1]), 0))
    one, zero = jnp.ones((), jnp.bfloat16), jnp.zeros((), jnp.bfloat16)
    return jnp.where(place == as_bf16(inside), one, zero), group


def kernel(
    tiles,
    mixing_hbm, counts_hbm, tracers_hbm, diffusion_hbm, coupling_hbm, source_hbm, mask_hbm, cells_hbm, areas_hbm,
    base_ref, slope_ref, flux_ref,
    tracers_ref, diffusion_ref, coupling_ref, source_ref, mask_ref, cells_ref, areas_ref, mixing_ref, counts_ref,
    load_sem,
    factor_ref, planes_ref, table_ref, table16_ref, own_ref, partner_ref, skin_ref, answer_ref, total_ref,
    edge_ref, halo_ref,
    send_sem, recv_sem, edge_send, edge_recv, word_sem,
):
    levels, fields, rows, lanes = tracers_ref.shape
    capacity = cells_ref.shape[1]
    halves = WIDE // lanes
    groups = rows * lanes // WIDE
    width = 2 * fields
    dense = capacity // 2
    comp = lax.axis_index("comp")
    tile = lax.axis_index("tile")
    other = 1 - comp
    after = lax.rem(tile + 1, tiles)
    before = lax.rem(tile + tiles - 1, tiles)

    side = tiles // 2
    place_in_side = tile % side
    near_base = (tile // side) * side
    far_base = side - near_base

    def near_block(j):
        return near_base + (place_in_side + j) % (side // 2) + (j // (side // 2)) * (side // 2)

    def in_order(first, i):
        part = side // 4
        return (place_in_side + 2 * part - first - 2 * (i % part)) % (2 * part) + (i // part) * 2 * part

    def asked_block(i):
        return far_base + in_order(comp, i)

    part = side // 4

    def owned_block(i):
        return far_base + (place_in_side + 1 - comp + 2 * (i % part)) % (2 * part) + (i // part) * 2 * part

    chunk = levels // CHUNKS

    def level_load(source, target, part, slot):
        span = pl.ds(part * chunk, chunk)
        return pltpu.make_async_copy(source.at[span], target.at[span], load_sem.at[slot])

    tracer_loads = [level_load(tracers_hbm, tracers_ref, c, c) for c in range(CHUNKS)]
    diffusion_loads = [level_load(diffusion_hbm, diffusion_ref, c, CHUNKS + c) for c in range(CHUNKS)]
    pairs = (
        (coupling_hbm, coupling_ref), (source_hbm, source_ref), (mask_hbm, mask_ref),
        (cells_hbm, cells_ref), (areas_hbm, areas_ref), (mixing_hbm, mixing_ref), (counts_hbm, counts_ref),
    )
    rest_loads = [
        pltpu.make_async_copy(held, target, load_sem.at[2 * CHUNKS + i]) for i, (held, target) in enumerate(pairs)
    ]
    for c in range(CHUNKS):
        diffusion_loads[c].start()
        if c >= 1:
            tracer_loads[c - 1].start()
    tracer_loads[CHUNKS - 1].start()
    for load in rest_loads:
        load.start()

    barrier = pltpu.get_barrier_semaphore()

    most = tiles - tiles // 4
    late = tile >= most
    prompt = tile < most
    has_before, has_after = tile > 0, tile < tiles - 1
    is_seam_low, is_seam_high = tile == most - 1, tile == most

    def greet(device_comp, block):
        pl.semaphore_signal(barrier, inc=1, device_id=(device_comp, block), device_id_type=MESH)

    def greet_all(device_comp, first, end):
        def step(block, carry):
            greet(device_comp, block)
            return carry

        lax.fori_loop(first, end, step, 0)

    @pl.when(prompt)
    def _():
        @pl.when(comp == 1)
        def _():
            greet_all(1, 0, tile)
            greet_all(1, tile + 1, most)

        @pl.when(comp == 0)
        def _():
            greet_all(1, 0, most)

        greet_all(other, most, tiles)

    @pl.when(late)
    def _():
        greet_all(0, 0, most)
        greet_all(other, most, tiles)

    @pl.when(jnp.logical_and(late, jnp.logical_not(is_seam_high)))
    def _():
        greet(comp, before)

    @pl.when(jnp.logical_and(tile >= most - 1, has_after))
    def _():
        greet(comp, after)

    def down(k, carry):
        factor, reduced = carry
        here = diffusion_ref[k]
        below = diffusion_ref[k + 1]
        field = tracers_ref[k]
        inverse = 1.0 / (1.0 + here + below - here * factor)
        factor = below * inverse
        reduced = (field + here * reduced) * inverse
        factor_ref[k] = factor
        base_ref[k] = reduced
        edge_ref[0, k] = field[:, rows - 1, :]
        edge_ref[1, k] = field[:, 0, :]
        return factor, reduced

    zeros = jnp.zeros((fields, rows, lanes), jnp.float32)
    factor, reduced = zeros, zeros
    diffusion_loads[0].wait()
    for c in range(CHUNKS):
        if c + 1 < CHUNKS:
            diffusion_loads[c + 1].wait()
        tracer_loads[c].wait()
        end = min((c + 1) * chunk, levels - 1)
        factor, reduced = lax.fori_loop(c * chunk, end, down, (factor, reduced), unroll=True)
    for load in rest_loads:
        load.wait()
    last = levels - 1
    here = diffusion_ref[last]
    field = tracers_ref[last]
    admittance = 1.0 / (1.0 + here - here * factor)
    bottom = (field + here * reduced) * admittance
    edge_ref[0, last] = field[:, rows - 1, :]
    edge_ref[1, last] = field[:, 0, :]
    base_ref[last] = bottom
    slope_ref[last] = admittance
    mask = mask_ref[...].astype(jnp.float32)[None]
    coupling = coupling_ref[...]
    conductance = mask * coupling / (1.0 + coupling * admittance)
    offered = mask * (source_ref[...] + conductance * bottom)
    for k in range(width):
        plane = offered[k] if k < fields else conductance[k - fields]
        for half in range(halves):
            table_ref[half, pl.ds(k, groups, stride=width), :] = plane[half * groups : (half + 1) * groups]
    table = jnp.concatenate([table_ref[half] for half in range(halves)], axis=1)
    high, low = split_two(table.reshape(groups, width, WIDE))
    table16_ref[...] = (
        jnp.concatenate([high, low], axis=1).reshape(groups * 2 * width, WIDE).astype(jnp.bfloat16)
    )

    edge_up = pltpu.make_async_remote_copy(
        src_ref=edge_ref.at[0], dst_ref=halo_ref.at[0], send_sem=edge_send.at[0], recv_sem=edge_recv.at[0],
        device_id=(comp, after), device_id_type=MESH,
    )
    edge_down = pltpu.make_async_remote_copy(
        src_ref=edge_ref.at[1], dst_ref=halo_ref.at[1], send_sem=edge_send.at[1], recv_sem=edge_recv.at[1],
        device_id=(comp, before), device_id_type=MESH,
    )
    def block_copy(block, slot):
        return pltpu.make_async_remote_copy(
            src_ref=own_ref.at[block], dst_ref=partner_ref.at[slot],
            send_sem=send_sem.at[block], recv_sem=recv_sem.at[slot],
            device_id=(other, block), device_id_type=MESH,
        )

    def answer_copy(block, slot):
        return pltpu.make_async_remote_copy(
            src_ref=skin_ref.at[block], dst_ref=answer_ref.at[slot],
            send_sem=send_sem.at[block], recv_sem=recv_sem.at[slot],
            device_id=(other, block), device_id_type=MESH,
        )

    def cells_of(block):
        return hot_of(cells_ref[pl.ds(block, 1), :], lanes, groups)

    def pick(blocks):
        hots, group = zip(*[cells_of(block) for block in blocks])
        found = jnp.dot(table16_ref[...], jnp.concatenate(hots, axis=1), preferred_element_type=jnp.float32)
        size = 2 * width
        chosen = [
            found[g * size : g * size + width] + found[g * size + width : (g + 1) * size] for g in range(groups)
        ]
        group = jnp.broadcast_to(jnp.concatenate(group, axis=1), (width, len(blocks) * capacity))
        stride = 1
        while len(chosen) > 1:
            odd = (group // stride) % 2 == 1
            chosen = [jnp.where(odd, chosen[i + 1], chosen[i]) for i in range(0, len(chosen), 2)]
            stride *= 2
        for i, block in enumerate(blocks):
            own_ref[block] = chosen[0][:, i * capacity : (i + 1) * capacity]

    def each(count, batch, block_of, do, first=0):
        def step(s, carry):
            do([block_of(first + s * batch + i) for i in range(batch)])
            return carry

        if count == batch:
            step(0, 0)
        else:
            lax.fori_loop(0, count // batch, step, 0)

    def pick_and_send(blocks):
        pick(blocks)
        for block in blocks:
            block_copy(block, tile).start()

    far_batch = min(BATCH, side // 2)
    near_batch = min(BATCH, side)
    near_half = min(BATCH, side // 2)
    part = side // 4
    ask_batch = min(BATCH, part)
    early = tile < side

    each(part, ask_batch, asked_block, pick)

    @pl.when(early)
    def _():
        each(part, ask_batch, asked_block, pick, first=part)

    def one_unless_zero(number):
        return (number + tiles - 1) // tiles

    @pl.when(jnp.logical_and(prompt, comp == 1))
    def _():
        pl.semaphore_wait(barrier, 2 * most - 1)
        pl.semaphore_signal(word_sem, inc=1, device_id=(other, tile), device_id_type=MESH)

    @pl.when(jnp.logical_and(prompt, comp == 0))
    def _():
        pl.semaphore_wait(word_sem, 1)

    @pl.when(late)
    def _():
        pl.semaphore_wait(barrier, tiles + 1 + one_unless_zero(tiles - 1 - tile))

    @pl.when(jnp.logical_and(has_after, jnp.logical_not(is_seam_low)))
    def _():
        edge_up.start()

    @pl.when(has_before)
    def _():
        edge_down.start()

    def send(step, carry):
        block_copy(asked_block(step), tile).start()
        return carry

    lax.fori_loop(0, part, send, 0)

    @pl.when(jnp.logical_not(early))
    def _():
        each(part, ask_batch, asked_block, pick, first=part)
        lax.fori_loop(part, 2 * part, send, 0)

    each(side // 2, near_half, near_block, pick_and_send)

    @pl.when(jnp.logical_not(early))
    def _():
        each(side // 2, far_batch, owned_block, pick)


    @pl.when(jnp.logical_and(prompt, comp == 0))
    def _():
        pl.semaphore_wait(barrier, 2 * (tiles - most))
        pl.semaphore_signal(word_sem, inc=1, device_id=(other, tile), device_id_type=MESH)

    @pl.when(jnp.logical_and(prompt, comp == 1))
    def _():
        pl.semaphore_wait(word_sem, 1)

    @pl.when(is_seam_low)
    def _():
        edge_up.start()

    @pl.when(early)
    def _():
        lax.fori_loop(part, 2 * part, send, 0)

    each(side // 2, near_half, near_block, pick_and_send, first=side // 2)

    @pl.when(early)
    def _():
        each(side // 2, far_batch, owned_block, pick)

    upper = lax.broadcasted_iota(jnp.int32, (width, dense), 0) < fields

    def skin_of(block):
        both = own_ref[block] + partner_ref[block]
        turned = pltpu.roll(both, fields, 0)
        offers = jnp.where(upper, both[:, :dense], turned[:, dense:])
        conducts = jnp.where(upper, turned[:, :dense], both[:, dense:])
        return offers / (conducts + 1.0)

    def answer(step, carry):
        block = owned_block(step)
        block_copy(block, block).wait_recv()
        skin_ref[block] = skin_of(block)
        answer_copy(block, tile).start()
        return carry

    def rise():
        @pl.when(has_after)
        def _():
            edge_up.wait_send()
            edge_down.wait_recv()

        @pl.when(has_before)
        def _():
            edge_down.wait_send()
            edge_up.wait_recv()

        @pl.when(tile == 0)
        def _():
            halo_ref[0] = jnp.zeros((levels, fields, lanes), jnp.float32)

        @pl.when(tile == tiles - 1)
        def _():
            halo_ref[1] = jnp.zeros((levels, fields, lanes), jnp.float32)

        row = lax.broadcasted_iota(jnp.int32, (fields, rows, lanes), 1)
        first_row = row == 0
        last_row = row == rows - 1
        which = lax.broadcasted_iota(jnp.int32, (fields, rows, lanes), 0)
        mix = jnp.zeros((fields, rows, lanes), jnp.float32)
        for f in range(fields):
            mix = jnp.where(which == f, mixing_ref[f], mix)

        def spread(k):
            field = tracers_ref[k]
            north = jnp.where(first_row, halo_ref[0, k][:, None, :], pltpu.roll(field, 1, 1))
            south = jnp.where(last_row, halo_ref[1, k][:, None, :], pltpu.roll(field, rows - 1, 1))
            along = pltpu.roll(field, 1, 2) + pltpu.roll(field, lanes - 1, 2)
            return mix * (north + south + along - 4.0 * field)

        base_ref[last] = bottom + spread(last)

        def up(step, carry):
            base, slope = carry
            k = levels - 2 - step
            factor = factor_ref[k]
            base = base_ref[k] + factor * base
            slope = factor * slope
            slope_ref[k] = slope
            base_ref[k] = base + spread(k)
            return base, slope

        lax.fori_loop(0, levels - 1, up, (bottom, admittance))

    @pl.when(early)
    def _():
        rise()

    lax.fori_loop(0, part, answer, 0)

    @pl.when(jnp.logical_not(early))
    def _():
        rise()

    lax.fori_loop(part, 2 * part, answer, 0)


    total_ref[...] = jnp.zeros_like(total_ref)
    slot_of = lax.broadcasted_iota(jnp.int32, (1, capacity), 1)
    group_of = as_bf16(lax.broadcasted_iota(jnp.int32, (groups, capacity), 0))

    def scatter(blocks, skins):
        hots, lefts = [], []
        for block, skin in zip(blocks, skins):
            hot, group = cells_of(block)
            here = group_of == as_bf16(group)
            area = jnp.where(slot_of < counts_ref[block], areas_ref[pl.ds(block, 1), :], 0.0)
            weight = skin * jnp.where(upper, area[:, :dense], area[:, dense:])
            pieces = []
            for part, area_part in zip(split_two(weight), split_two(area)):
                found = [
                    jnp.concatenate([part[f : f + 1], part[fields + f : fields + f + 1]], axis=1)
                    for f in range(fields)
                ]
                for value in found + [area_part]:
                    spread_value = jnp.broadcast_to(value, (groups, capacity)).astype(jnp.bfloat16)
                    pieces.append(jnp.where(here, spread_value, jnp.zeros((), jnp.bfloat16)))
            hots.append(hot)
            lefts.append(jnp.concatenate(pieces, axis=0))
        total_ref[...] += lax.dot_general(
            jnp.concatenate(hots, axis=1), jnp.concatenate(lefts, axis=1), (((1,), (1,)), ((), ())),
            preferred_element_type=jnp.float32,
        )

    def scatter_owned(blocks):
        scatter(blocks, [skin_ref[block] for block in blocks])

    def scatter_near(blocks):
        for block in blocks:
            block_copy(block, block).wait_recv()
        scatter(blocks, [skin_of(block) for block in blocks])

    def scatter_asked(blocks):
        for block in blocks:
            answer_copy(block, block).wait_recv()
        scatter(blocks, [answer_ref[block] for block in blocks])

    each(side // 2, far_batch, owned_block, scatter_owned)
    each(side, near_batch, near_block, scatter_near)
    each(side // 2, 2, asked_block, scatter_asked)

    sums = (fields + 1) * groups
    totals = total_ref[...].T
    totals = totals[:sums] + totals[sums:]
    for k in range(fields + 1):
        for half in range(halves):
            planes_ref[k, half * groups : (half + 1) * groups, :] = totals[
                k * groups : (k + 1) * groups, half * lanes : (half + 1) * lanes
            ]
    flux_ref[...] = conductance * (planes_ref[0:fields] - bottom * planes_ref[fields : fields + 1])

    def drain(step, carry):
        block_copy(asked_block(step), tile).wait_send()
        answer_copy(owned_block(step), tile).wait_send()
        return carry

    def drain_near(step, carry):
        block_copy(near_block(step), tile).wait_send()
        return carry

    lax.fori_loop(0, side // 2, drain, 0)
    lax.fori_loop(0, side, drain_near, 0)


def finish(base_ref, slope_ref, flux_ref, solved_hbm, surface_hbm, solved_ref, store_sem):
    chunk = base_ref.shape[0] // CHUNKS
    flux_store = pltpu.make_async_copy(flux_ref, surface_hbm, store_sem.at[CHUNKS])
    flux_store.start()
    flux = flux_ref[...]
    stores = []
    for c in range(CHUNKS):
        span = pl.ds(c * chunk, chunk)

        def combine(k, carry):
            solved_ref[k] = base_ref[k] + slope_ref[k] * flux
            return carry

        lax.fori_loop(c * chunk, (c + 1) * chunk, combine, 0, unroll=True)
        stores.append(pltpu.make_async_copy(solved_ref.at[span], solved_hbm.at[span], store_sem.at[c]))
        stores[-1].start()
    flux_store.wait()
    for store in stores:
        store.wait()


def on_device(
    tracers, diffusion, coupling, source, sea_mask, mixing, cell_counts, cell_columns, cell_areas
):
    levels, fields, rows, lanes = tracers.shape[1:]
    tiles, capacity = cell_columns.shape[2:]
    width = 2 * fields
    groups = rows * lanes // WIDE
    f32 = jnp.float32
    grid = jax.ShapeDtypeStruct((levels, fields, rows, lanes), f32)
    vmem = pl.BlockSpec(memory_space=pltpu.VMEM)
    held = [
        pltpu.with_memory_space_constraint(array, pltpu.HBM)
        for array in (
            tracers[0], diffusion[0], coupling[0], source[0], sea_mask[0], cell_columns[0, 0], cell_areas[0, 0]
        )
    ]
    base, slope, flux = pl.pallas_call(
        functools.partial(kernel, tiles),
        out_shape=(grid, grid, jax.ShapeDtypeStruct((fields, rows, lanes), f32)),
        in_specs=[pl.BlockSpec(memory_space=pltpu.HBM)] * 9,
        out_specs=(vmem, vmem, vmem),
        scratch_shapes=[
            pltpu.VMEM((levels, fields, rows, lanes), f32),
            pltpu.VMEM((levels, fields, rows, lanes), f32),
            pltpu.VMEM((fields, rows, lanes), f32),
            pltpu.VMEM((fields, rows, lanes), f32),
            pltpu.VMEM((rows, lanes), jnp.int32),
            pltpu.VMEM((tiles, capacity), jnp.int32),
            pltpu.VMEM((tiles, capacity), f32),
            pltpu.SMEM((fields,), f32),
            pltpu.SMEM((tiles,), jnp.int32),
            pltpu.SemaphoreType.DMA((2 * CHUNKS + 7,)),
            pltpu.VMEM((levels, fields, rows, lanes), f32),
            pltpu.VMEM((fields + 1, rows, lanes), f32),
            pltpu.VMEM((WIDE // lanes, groups * width, lanes), f32),
            pltpu.VMEM((groups * 2 * width, WIDE), jnp.bfloat16),
            pltpu.VMEM((tiles, width, capacity), f32),
            pltpu.VMEM((tiles, width, capacity), f32),
            pltpu.VMEM((tiles, width, capacity // 2), f32),
            pltpu.VMEM((tiles, width, capacity // 2), f32),
            pltpu.VMEM((WIDE, 2 * (fields + 1) * groups), f32),
            pltpu.VMEM((2, levels, fields, lanes), f32),
            pltpu.VMEM((2, levels, fields, lanes), f32),
            pltpu.SemaphoreType.DMA((tiles,)),
            pltpu.SemaphoreType.DMA((tiles,)),
            pltpu.SemaphoreType.DMA((2,)),
            pltpu.SemaphoreType.DMA((2,)),
            pltpu.SemaphoreType.REGULAR,
        ],
        compiler_params=pltpu.CompilerParams(
            collective_id=0, has_side_effects=True, vmem_limit_bytes=48 << 20
        ),
    )(
        pltpu.with_memory_space_constraint(mixing[0], pltpu.HBM),
        pltpu.with_memory_space_constraint(cell_counts[0, 0], pltpu.HBM), *held,
    )
    hbm = pl.BlockSpec(memory_space=pltpu.HBM)
    solved, surface = pl.pallas_call(
        finish,
        out_shape=(grid, jax.ShapeDtypeStruct((fields, rows, lanes), f32)),
        in_specs=[vmem, vmem, vmem],
        out_specs=(hbm, hbm),
        scratch_shapes=[
            pltpu.VMEM((levels, fields, rows, lanes), f32),
            pltpu.SemaphoreType.DMA((CHUNKS + 1,)),
        ],
        compiler_params=pltpu.CompilerParams(vmem_limit_bytes=8 << 20),
    )(base, slope, flux)
    return (solved[None], surface[None])


def solution(mesh):
    in_specs = (
        P("comp", None, None, "tile", None),
        P("comp", None, None, "tile", None),
        P("comp", None, "tile", None),
        P("comp", None, "tile", None),
        P("comp", "tile", None),
        P("comp", None),
        P("comp", "tile", None),
        P("comp", "tile", None, None),
        P("comp", "tile", None, None),
    )
    out_specs = (P("comp", None, None, "tile", None), P("comp", None, "tile", None))
    return jax.shard_map(
        on_device, mesh=mesh, in_specs=in_specs, out_specs=out_specs, check_vma=False
    )
```
